256 devices in a mesh: group: 8 (over z_hi, core), tensor: 8 (over y, z_lo), seq: 4 (over x).
Axes of the slice: x: 4, y: 4, z: 8 (z_hi: 4, z_lo: 2; z = z_hi * 2 + z_lo), core: 2. Of those that a mesh axis runs over, the one named last changes fastest.
Arguments:
- patches: bfloat16 [8192, 1280], P(('group', 'tensor', 'seq')), may hold values from -6 to 6
- enc_gain: float32 [1280], replicated, may hold values from 0.1 to 1.9
- enc_qkv: bfloat16 [3, 1280, 1280], P(None, None, 'tensor')
- enc_out: bfloat16 [1280, 1280], P('tensor'), may hold values from -0.15625 to 0.15625
- cross_kv: bfloat16 [1280, 2048], P(None, 'tensor'), may hold values from -0.15625 to 0.15625
- key_gain: float32 [128], replicated, may hold values from 0.1 to 1.9
- dec_hidden: bfloat16 [4096, 8192], P(('group', 'seq')), may hold values from -6 to 6
- dec_gain: float32 [8192], replicated, may hold values from 0.1 to 1.9
- query_weight: bfloat16 [8192, 4096], P(None, 'tensor'), may hold values from -0.0625 to 0.0625
- query_gain: float32 [128], replicated, may hold values from 1.5 to 3
- image_of_row: int32 [4096], P(('group', 'seq')), may hold values from 0 to 3
- valid_count: int32 [4096], P(('group', 'seq')), may hold values from 1 to 2048, as said below
Outputs:
- decoded: bfloat16 [4096, 4096], P(('group', 'seq'), 'tensor')
The draws below stay inside these ranges and needn't reach their ends.
Inputs may be any that keep to these rules, and one draw needn't show every extreme that they name: `valid_count`: every draw has a row reading a whole image and a row reading one patch.
All inputs are finite; a program needn't handle non-finite values.
Results may differ from the reference program's by a relative error of at most 0.028.
The reference program's roundings to bfloat16 on the way (of `normed`, `attended`, `encoded`, `dec_normed` and `queries`) count: a program that leaves them out, or rounds other values in their place, can miss the bound.
Values may be sent and summed in bfloat16 or wider, within the bound.
No kernel may reach another device: no remote copies, remote signals or barrier semaphores. Data moves between devices by JAX's collectives and lax.ppermute only.
A program may use at most 128 MiB of HBM per device.

```python
import math
import jax
import jax.numpy as jnp
from jax import lax

VD = 1280
EH = 16
EHD = 80
D = 8192
H = 32
KVH = 8
HD = 128
IMAGES = 4
PATCHES = 8192
IMG_PATCH = 2048
BLOCK = 128
ROWS = 4096


def draw_enc_qkv(key, part):
    weights = jax.random.normal(key, (3, VD, VD), jnp.float32) * VD ** (-0.5)
    scaling = jnp.array([2.0, 2.0, 1.0], jnp.float32).reshape(3, 1, 1)
    weights = weights * scaling
    return weights.astype(jnp.bfloat16)


def draw_valid_count(key, part):
    first_key, second_key, third_key, fourth_key = jax.random.split(key, 4)
    image_patches = PATCHES // IMAGES
    bounds = jax.random.randint(fourth_key, (ROWS,), 1, image_patches + 1, dtype=jnp.int32)
    counts = jax.random.randint(first_key, (ROWS,), 1, bounds + 1, dtype=jnp.int32)
    spot_high = jax.random.randint(second_key, (), 0, ROWS, dtype=jnp.int32)
    offset_low = jax.random.randint(third_key, (), 1, ROWS, dtype=jnp.int32)
    spot_low = (spot_high + offset_low) % ROWS
    counts = counts.at[spot_high].set(image_patches)
    counts = counts.at[spot_low].set(1)
    return counts


def plant(values, rng, low, largest):
    index_at = [jax.random.randint(jax.random.fold_in(rng, axis), (), 0, length) for axis, length in enumerate(values.shape)]
    main_axis = values.shape.index(max(values.shape))
    neighbour = index_at[:main_axis] + [(index_at[main_axis] + 1) % values.shape[main_axis]] + index_at[main_axis + 1:]
    return values.at[tuple(index_at)].set(low).at[tuple(neighbour)].set(largest)


def block_levels(own_key, dims, cuts, low, top_value):
    gain, own = 1.0, jax.random.fold_in(own_key, 6)
    for position, parts in cuts:
        heights = jnp.exp(jax.random.uniform(jax.random.fold_in(own, position), (parts,), jnp.float32, low / len(cuts), top_value / len(cuts)))
        gain = gain * jnp.repeat(heights, dims[position] // parts).reshape([-1 if axis == position else 1 for axis in range(len(dims))])
    return gain


def centred(key, shape, deviation, most, pieces=(), kind=jnp.bfloat16):
    values = deviation * jax.random.normal(key, shape, jnp.float32)
    if pieces:
        values = values * block_levels(key, shape, pieces, -0.22, 0.18)
    return jnp.clip(values, -most, most).astype(kind)


def setup_inputs(seed: int = 0) -> dict:
    keys = jax.random.split(jax.random.key(seed), 13)
    patches = centred(keys[0], (PATCHES, VD), 1.0, 6.0, ((0, 256),))
    enc_gain = jnp.clip(1.0 + 0.18 * jax.random.normal(keys[1], (VD,), jnp.float32), 0.1, 1.9)
    enc_qkv = draw_enc_qkv(jax.random.fold_in(keys[12], 71), 0)
    enc_out = centred(keys[3], (VD, VD), VD ** -0.5, 0.15625, ((0, 8),))
    cross_kv = centred(keys[4], (VD, KVH * 2 * HD), VD ** -0.5, 0.15625, ((1, 8),))
    key_gain = jnp.clip(1.0 + 0.18 * jax.random.normal(keys[5], (HD,), jnp.float32), 0.1, 1.9)
    dec_hidden = centred(keys[6], (ROWS, D), 1.0, 6.0, ((0, 32),))
    dec_gain = jnp.clip(1.0 + 0.18 * jax.random.normal(keys[7], (D,), jnp.float32), 0.1, 1.9)
    query_weight = centred(keys[8], (D, H * HD), D ** -0.5, 0.0625, ((1, 8),))
    query_gain = jnp.clip(jax.random.uniform(keys[9], (HD,), jnp.float32, 1.5, 3.0), 1.5, 3.0)
    image_of_row = plant(jax.random.randint(keys[10], (ROWS,), 0, IMAGES), jax.random.fold_in(keys[10], 1), 0, IMAGES - 1).astype(jnp.int32)
    valid_count = draw_valid_count(jax.random.fold_in(keys[12], 71), 0)
    return dict(patches=patches, enc_gain=enc_gain, enc_qkv=enc_qkv, enc_out=enc_out, cross_kv=cross_kv, key_gain=key_gain, dec_hidden=dec_hidden, dec_gain=dec_gain, query_weight=query_weight, query_gain=query_gain, image_of_row=image_of_row, valid_count=valid_count)


EPSILON = 1e-05

def layer_norm(values, gain_vector):
    mean_value = lax.optimization_barrier(jnp.mean(values, axis=-1, keepdims=True))
    centered = values - mean_value
    variance = lax.optimization_barrier(jnp.mean(centered * centered, axis=-1, keepdims=True))
    return centered * lax.rsqrt(variance + EPSILON) * gain_vector

def rms_norm(values, gain_vector):
    square_mean = lax.optimization_barrier(jnp.mean(values * values, axis=-1, keepdims=True))
    return values * lax.rsqrt(square_mean + EPSILON) * gain_vector

def to_images(values):
    rounds = PATCHES // (IMAGES * BLOCK)
    return values.reshape(rounds, IMAGES, BLOCK, EHD).transpose(1, 0, 2, 3).reshape(IMAGES, IMG_PATCH, EHD)

def from_images(values):
    rounds = PATCHES // (IMAGES * BLOCK)
    return values.reshape(IMAGES, rounds, BLOCK, EHD).transpose(1, 0, 2, 3).reshape(PATCHES, EHD)

def encoder_head(query_head, key_head, value_head):
    block_rows = math.gcd(IMG_PATCH, 1024)
    query_images = to_images(query_head)
    key_images = to_images(key_head)
    value_images = to_images(value_head)

    def one_image(triple):
        image_query, image_key, image_value = triple
        query_blocks = image_query.reshape(IMG_PATCH // block_rows, block_rows, EHD)

        def one_block(query_block):
            scores = jnp.dot(query_block, image_key.T, preferred_element_type=jnp.float32) / math.sqrt(EHD)
            row_max = lax.optimization_barrier(jnp.max(scores, axis=-1, keepdims=True))
            weights = jnp.exp(scores - row_max)
            weight_sum = lax.optimization_barrier(jnp.sum(weights, axis=-1, keepdims=True))
            mixture = jnp.dot(weights.astype(jnp.bfloat16), image_value, preferred_element_type=jnp.float32)
            return (mixture / weight_sum).astype(jnp.bfloat16)
        return lax.map(one_block, query_blocks).reshape(IMG_PATCH, EHD)
    return from_images(lax.map(one_image, (query_images, key_images, value_images)))

def reference(patches, enc_gain, enc_qkv, enc_out, cross_kv, key_gain, dec_hidden, dec_gain, query_weight, query_gain, image_of_row, valid_count):
    normed = layer_norm(patches.astype(jnp.float32), enc_gain).astype(jnp.bfloat16)

    def project(which):
        result = jnp.dot(normed, enc_qkv[which], preferred_element_type=jnp.float32).astype(jnp.bfloat16)
        return result.reshape(PATCHES, EH, EHD).transpose(1, 0, 2)
    query_all = project(0)
    key_all = project(1)
    value_all = project(2)
    attended = lax.map(lambda triple: encoder_head(triple[0], triple[1], triple[2]), (query_all, key_all, value_all))
    attended = attended.transpose(1, 0, 2).reshape(PATCHES, VD)
    encoded = (patches.astype(jnp.float32) + jnp.dot(attended, enc_out, preferred_element_type=jnp.float32)).astype(jnp.bfloat16)
    cross_proj = jnp.dot(encoded, cross_kv, preferred_element_type=jnp.float32).reshape(PATCHES, KVH, 2, HD)
    cross_keys = rms_norm(cross_proj[:, :, 0], key_gain).astype(jnp.bfloat16)
    cross_values = cross_proj[:, :, 1].astype(jnp.bfloat16)
    dec_normed = rms_norm(dec_hidden.astype(jnp.float32), dec_gain).astype(jnp.bfloat16)
    queries = jnp.dot(dec_normed, query_weight, preferred_element_type=jnp.float32).reshape(ROWS, H, HD)
    queries = (rms_norm(queries, query_gain) / math.sqrt(HD)).astype(jnp.bfloat16)
    positions = jnp.arange(PATCHES, dtype=jnp.int32)
    patch_image = positions // BLOCK % IMAGES
    patch_pos = positions // (BLOCK * IMAGES) * BLOCK + positions % BLOCK
    allowed = (patch_image[None, :] == image_of_row[:, None]) & (patch_pos[None, :] < valid_count[:, None])

    def one_head(head_index):
        query_head = lax.dynamic_index_in_dim(queries, head_index, 1, keepdims=False)
        kv_index = head_index // (H // KVH)
        key_head = lax.dynamic_index_in_dim(cross_keys, kv_index, 1, keepdims=False)
        value_head = lax.dynamic_index_in_dim(cross_values, kv_index, 1, keepdims=False)
        scores = jnp.dot(query_head, key_head.T, preferred_element_type=jnp.float32)
        weights = jnp.where(allowed, jnp.exp(scores), jnp.zeros_like(scores))
        weight_sum = lax.optimization_barrier(jnp.sum(weights, axis=-1, keepdims=True))
        mixture = jnp.dot(weights.astype(jnp.bfloat16), value_head, preferred_element_type=jnp.float32) / weight_sum
        return mixture.astype(jnp.bfloat16)
    heads_out = lax.map(one_head, jnp.arange(H, dtype=jnp.int32))
    return heads_out.transpose(1, 0, 2).reshape(ROWS, H * HD)
```

```python
import math

import jax
import jax.numpy as jnp
from jax import lax
from jax.experimental import pallas as pl
from jax.experimental.pallas import tpu as pltpu
from jax.sharding import Mesh
from jax.sharding import PartitionSpec as P

EHD = 80
HD = 128
EPSILON = 1e-05
F32 = jnp.float32
BF16 = jnp.bfloat16
ZH, CORES, YS, ZL, XS = 4, 2, 4, 2, 4
TENSOR = YS * ZL
NT = (((1,), (1,)), ((), ()))


def rms_norm(values, gain_vector):
    square_mean = jnp.mean(values * values, axis=-1, keepdims=True)
    return values * lax.rsqrt(square_mean + EPSILON) * gain_vector


def vmem(count):
    return [pl.BlockSpec(memory_space=pltpu.VMEM)] * count


def smem():
    return pl.BlockSpec(memory_space=pltpu.SMEM)


def xor_permute(values, axes, size, step):
    return lax.ppermute(values, axes, [(i, i ^ step) for i in range(size)])


def image_permute(values):
    pairs = []
    for zh in range(ZH):
        for y in range(YS):
            for zl in range(ZL):
                image, slot = (y % 2) * 2 + zl, zh * 2 + y // 2
                pairs.append(((zh * YS + y) * ZL + zl, image * TENSOR + slot))
    return lax.ppermute(values, ("zh", "y", "zl"), pairs)


def qkv_kernel(me_ref, *refs):
    pieces, (gain_ref, weight_ref, q_ref, kv_ref, normed) = refs[:TENSOR], refs[TENSOR:]
    me = me_ref[0]
    for step in range(TENSOR):
        values = pieces[step][...].astype(F32)
        mean_value = jnp.mean(values, axis=-1, keepdims=True)
        centered = values - mean_value
        variance = jnp.mean(centered * centered, axis=-1, keepdims=True)
        result = centered * lax.rsqrt(variance + EPSILON) * gain_ref[...]
        rows = values.shape[0]
        slot = jnp.bitwise_xor(me, step)
        normed[pl.ds(pl.multiple_of(slot * rows, rows), rows), :] = result.astype(BF16)
    x = normed[...]
    q = jnp.dot(x, weight_ref[0], preferred_element_type=F32)
    for head in range(2):
        q_ref[head] = q[:, head * EHD : (head + 1) * EHD].astype(BF16)
    width = 2 * EHD
    for part in range(2):
        out = jnp.dot(x, weight_ref[1 + part], preferred_element_type=F32)
        kv_ref[part * width : (part + 1) * width, :] = out.T.astype(BF16)


def encoder_kernel(q_ref, *refs):
    count = 8
    pieces, (weight_ref, out_ref, scores) = refs[:count], refs[count:]
    rows = q_ref.shape[1]
    scale = 1.0 / math.sqrt(EHD)
    heads = []
    for head in range(2):
        q = q_ref[head]
        top = None
        for j in range(count):
            s = jnp.dot(q, pieces[j][head * EHD : (head + 1) * EHD, :], preferred_element_type=F32)
            scores[head, :, j * rows : (j + 1) * rows] = s
            part = jnp.maximum(s[:, :128], s[:, 128:])
            top = part if top is None else jnp.maximum(top, part)
        top = jnp.max(top, axis=-1, keepdims=True)
        mix = jnp.zeros((rows, EHD), F32)
        total = jnp.zeros((rows, 128), F32)
        low = 2 * EHD + head * EHD
        for j in range(count):
            p = jnp.exp((scores[head, :, j * rows : (j + 1) * rows] - top) * scale)
            total = total + (p[:, :128] + p[:, 128:])
            mix = mix + lax.dot_general(
                p.astype(BF16), pieces[j][low : low + EHD, :], NT, preferred_element_type=F32
            )
        heads.append((mix / jnp.sum(total, axis=-1, keepdims=True)).astype(BF16))
    partial = jnp.dot(heads[0], weight_ref[:EHD, :], preferred_element_type=F32)
    partial = partial + jnp.dot(heads[1], weight_ref[EHD:, :], preferred_element_type=F32)
    size = rows // TENSOR
    for slot in range(TENSOR):
        out_ref[slot] = partial[slot * size : (slot + 1) * size].astype(BF16)


def cross_kernel(me_ref, *refs):
    pieces, (weight_ref, gain_ref, out_ref, encoded) = refs[:TENSOR], refs[TENSOR:]
    me = me_ref[0]
    for step in range(TENSOR):
        rows = pieces[step].shape[0]
        slot = jnp.bitwise_xor(me, step)
        encoded[pl.ds(pl.multiple_of(slot * rows, rows), rows), :] = pieces[step][...]
    proj = jnp.dot(encoded[...], weight_ref[...], preferred_element_type=F32)
    keys = proj[:, :HD]
    square_mean = jnp.mean(keys * keys, axis=-1, keepdims=True)
    keys = keys * lax.rsqrt(square_mean + EPSILON) * gain_ref[...]
    out_ref[:, :HD] = keys.astype(BF16)
    out_ref[:, HD:] = proj[:, HD:].astype(BF16)


def decode_kernel(place_ref, *refs):
    queries, refs = refs[:ZH], refs[ZH:]
    slabs, refs = refs[:8], refs[8:]
    outs = refs[:ZH]
    rows = queries[0].shape[0]
    keys = slabs[0].shape[0]
    zh, x, c = place_ref[0], place_ref[1], place_ref[2]
    lane = lax.broadcasted_iota(jnp.int32, (1, keys), 1)
    base = (lane >> 6) * 512 + ((lane >> 5) & 1) * 128 + (lane & 31)
    here = zh.astype(F32)
    for k in range(ZH):
        extra = queries[k][:, 4 * HD :].astype(F32)
        limit = extra[:, 1:2] * 16.0 + extra[:, 2:3]
        limit = jnp.where(extra[:, 0:1] == here, limit, 0.0)
        for head in range(4):
            q = queries[k][:, head * HD : (head + 1) * HD]
            mix = jnp.zeros((rows, HD), F32)
            total = jnp.zeros((rows, 128), F32)
            for j in range(8):
                px = jnp.bitwise_xor(x, j % 4)
                pc = jnp.bitwise_xor(c, j // 4)
                pos = (base + (pc * 256 + px * 32)).astype(F32)
                s = lax.dot_general(q, slabs[j][:, :HD], NT, preferred_element_type=F32)
                w = jnp.where(pos < limit, jnp.exp(s), 0.0)
                total = total + (w[:, :128] + w[:, 128:])
                mix = mix + jnp.dot(w.astype(BF16), slabs[j][:, HD:], preferred_element_type=F32)
            total = jnp.sum(total, axis=-1, keepdims=True)
            total = jnp.where(total > 0.0, total, 1.0)
            outs[k][:, head * HD : (head + 1) * HD] = (mix / total).astype(BF16)


def gather_xc(piece):
    along_x = [piece] + [xor_permute(piece, "x", XS, k) for k in range(1, XS)]
    return along_x + [xor_permute(value, "c", CORES, 1) for value in along_x]


def gather_tensor(piece):
    return [piece] + [xor_permute(piece, ("y", "zl"), TENSOR, k) for k in range(1, TENSOR)]


def on_device(
    patches,
    enc_gain,
    enc_qkv,
    enc_out,
    cross_kv,
    key_gain,
    dec_hidden,
    dec_gain,
    query_weight,
    query_gain,
    image_of_row,
    valid_count,
):
    tensor_index = (lax.axis_index("y") * ZL + lax.axis_index("zl")).astype(jnp.int32)
    me = tensor_index.reshape(1)
    place = jnp.stack([lax.axis_index("zh"), lax.axis_index("x"), lax.axis_index("c")]).astype(
        jnp.int32
    )
    patch_rows, width = patches.shape
    rows = patch_rows * TENSOR
    own = image_permute(patches)

    dec_rows = dec_hidden.shape[0]
    dec_normed = rms_norm(dec_hidden.astype(F32), dec_gain).astype(BF16)
    queries = jnp.dot(dec_normed, query_weight, preferred_element_type=F32)
    queries = queries.reshape(dec_rows, -1, HD)
    queries = (rms_norm(queries, query_gain) / math.sqrt(HD)).astype(BF16)
    columns = jnp.stack([image_of_row, valid_count // 16, valid_count % 16], axis=1).astype(BF16)
    message = jnp.concatenate(
        [queries.reshape(dec_rows, -1), jnp.pad(columns, ((0, 0), (0, HD - 3)))], axis=1
    )

    pieces = gather_tensor(own)
    q, kv = pl.pallas_call(
        qkv_kernel,
        out_shape=(
            jax.ShapeDtypeStruct((2, rows, EHD), BF16),
            jax.ShapeDtypeStruct((4 * EHD, rows), BF16),
        ),
        in_specs=[smem()] + vmem(TENSOR + 2),
        out_specs=tuple(vmem(2)),
        scratch_shapes=[pltpu.VMEM((rows, width), BF16)],
    )(me, *pieces, enc_gain.reshape(1, -1), enc_qkv)
    kv_pieces = gather_xc(kv)
    every_query = [message] + [xor_permute(message, "zh", ZH, k) for k in range(1, ZH)]

    partial = pl.pallas_call(
        encoder_kernel,
        out_shape=jax.ShapeDtypeStruct((TENSOR, patch_rows, width), BF16),
        in_specs=vmem(10),
        out_specs=vmem(1)[0],
        scratch_shapes=[pltpu.VMEM((2, rows, 8 * rows), F32)],
    )(q, *kv_pieces, enc_out)
    shares = lax.all_to_all(partial, ("y", "zl"), 0, 0)
    encoded = (own.astype(F32) + jnp.sum(shares.astype(F32), axis=0)).astype(BF16)
    slab = pl.pallas_call(
        cross_kernel,
        out_shape=jax.ShapeDtypeStruct((rows, 2 * HD), BF16),
        in_specs=[smem()] + vmem(TENSOR + 2),
        out_specs=vmem(1)[0],
        scratch_shapes=[pltpu.VMEM((rows, width), BF16)],
    )(me, *gather_tensor(encoded), cross_kv, key_gain.reshape(1, -1))
    slabs = gather_xc(slab)
    outs = pl.pallas_call(
        decode_kernel,
        out_shape=tuple([jax.ShapeDtypeStruct((dec_rows, 4 * HD), BF16)] * ZH),
        in_specs=[smem()] + vmem(ZH + 8),
        out_specs=tuple(vmem(ZH)),
    )(place, *every_query, *slabs)
    result = outs[0]
    for k in range(1, ZH):
        result = result + xor_permute(outs[k], "zh", ZH, k)
    return result


def solution(mesh):
    parts = Mesh(mesh.devices.reshape(ZH, CORES, YS, ZL, XS), ("zh", "c", "y", "zl", "x"))
    group, tensor, seq = ("zh", "c"), ("y", "zl"), ("x",)
    in_specs = (
        P(group + tensor + seq, None),
        P(),
        P(None, None, tensor),
        P(tensor, None),
        P(None, tensor),
        P(),
        P(group + seq, None),
        P(),
        P(None, tensor),
        P(),
        P(group + seq),
        P(group + seq),
    )
    out_specs = P(group + seq, tensor)
    return jax.shard_map(
        on_device, mesh=parts, in_specs=in_specs, out_specs=out_specs, check_vma=False
    )
```

```python
import math

import jax
import jax.numpy as jnp
from jax import lax
from jax.experimental import pallas as pl
from jax.experimental.pallas import tpu as pltpu
from jax.sharding import Mesh
from jax.sharding import PartitionSpec as P

EHD = 80
HD = 128
EPSILON = 1e-05
F32 = jnp.float32
BF16 = jnp.bfloat16
ZH, CORES, YS, ZL, XS = 4, 2, 4, 2, 4
TENSOR = YS * ZL
NT = (((1,), (1,)), ((), ()))


def rms_norm(values, gain_vector):
    square_mean = jnp.mean(values * values, axis=-1, keepdims=True)
    return values * lax.rsqrt(square_mean + EPSILON) * gain_vector


def vmem(count):
    return [pl.BlockSpec(memory_space=pltpu.VMEM)] * count


def smem():
    return pl.BlockSpec(memory_space=pltpu.SMEM)


def xor_permute(values, axes, size, step):
    return lax.ppermute(values, axes, [(i, i ^ step) for i in range(size)])


def image_permute(values):
    pairs = []
    for zh in range(ZH):
        for y in range(YS):
            for zl in range(ZL):
                image, slot = (y % 2) * 2 + zl, zh * 2 + y // 2
                pairs.append(((zh * YS + y) * ZL + zl, image * TENSOR + slot))
    return lax.ppermute(values, ("zh", "y", "zl"), pairs)


def qkv_kernel(me_ref, *refs):
    pieces, (gain_ref, weight_ref, q_ref, kv_ref, normed) = refs[:TENSOR], refs[TENSOR:]
    me = me_ref[0]
    for step in range(TENSOR):
        values = pieces[step][...].astype(F32)
        mean_value = jnp.mean(values, axis=-1, keepdims=True)
        centered = values - mean_value
        variance = jnp.mean(centered * centered, axis=-1, keepdims=True)
        result = centered * lax.rsqrt(variance + EPSILON) * gain_ref[...]
        rows = values.shape[0]
        slot = jnp.bitwise_xor(me, step)
        normed[pl.ds(pl.multiple_of(slot * rows, rows), rows), :] = result.astype(BF16)
    x = normed[...]
    q = lax.dot_general(x, weight_ref[0], NT, preferred_element_type=F32)
    for head in range(2):
        q_ref[head] = q[:, head * EHD : (head + 1) * EHD].astype(BF16)
    width = 2 * EHD
    for part in range(2):
        out = lax.dot_general(weight_ref[1 + part], x, NT, preferred_element_type=F32)
        kv_ref[part * width : (part + 1) * width, :] = out.astype(BF16)


def encoder_kernel(q_ref, *refs):
    count = 8
    pieces, (weight_ref, out_ref, scores) = refs[:count], refs[count:]
    rows = q_ref.shape[1]
    scale = 1.0 / math.sqrt(EHD)
    heads = []
    for head in range(2):
        q = q_ref[head]
        top = None
        for j in range(count):
            s = jnp.dot(q, pieces[j][head * EHD : (head + 1) * EHD, :], preferred_element_type=F32)
            scores[head, :, j * rows : (j + 1) * rows] = s
            part = jnp.maximum(s[:, :128], s[:, 128:])
            top = part if top is None else jnp.maximum(top, part)
        top = jnp.max(top, axis=-1, keepdims=True)
        mix = jnp.zeros((rows, EHD), F32)
        total = jnp.zeros((rows, 128), F32)
        low = 2 * EHD + head * EHD
        for j in range(count):
            p = jnp.exp((scores[head, :, j * rows : (j + 1) * rows] - top) * scale)
            total = total + (p[:, :128] + p[:, 128:])
            mix = mix + lax.dot_general(
                p.astype(BF16), pieces[j][low : low + EHD, :], NT, preferred_element_type=F32
            )
        heads.append((mix / jnp.sum(total, axis=-1, keepdims=True)).astype(BF16))
    partial = jnp.dot(heads[0], weight_ref[:EHD, :], preferred_element_type=F32)
    partial = partial + jnp.dot(heads[1], weight_ref[EHD:, :], preferred_element_type=F32)
    size = rows // TENSOR
    for slot in range(TENSOR):
        out_ref[slot] = partial[slot * size : (slot + 1) * size].astype(BF16)


def cross_kernel(me_ref, *refs):
    pieces, (weight_ref, gain_ref, out_ref, encoded) = refs[:TENSOR], refs[TENSOR:]
    me = me_ref[0]
    for step in range(TENSOR):
        rows = pieces[step].shape[0]
        slot = jnp.bitwise_xor(me, step)
        encoded[pl.ds(pl.multiple_of(slot * rows, rows), rows), :] = pieces[step][...]
    proj = jnp.dot(encoded[...], weight_ref[...], preferred_element_type=F32)
    keys = proj[:, :HD]
    square_mean = jnp.mean(keys * keys, axis=-1, keepdims=True)
    keys = keys * lax.rsqrt(square_mean + EPSILON) * gain_ref[...]
    out_ref[:, :HD] = keys.astype(BF16)
    out_ref[:, HD:] = proj[:, HD:].astype(BF16)


def decode_kernel(place_ref, query_ref, *refs):
    slabs, out_ref = refs[:8], refs[8]
    rows = query_ref.shape[0]
    keys = slabs[0].shape[0]
    zh, x, c = place_ref[0], place_ref[1], place_ref[2]
    lane = lax.broadcasted_iota(jnp.int32, (1, keys), 1)
    base = (lane >> 6) * 512 + ((lane >> 5) & 1) * 128 + (lane & 31)
    extra = query_ref[:, 4 * HD :].astype(F32)
    limit = extra[:, 1:2] * 16.0 + extra[:, 2:3]
    limit = jnp.where(extra[:, 0:1] == zh.astype(F32), limit, 0.0)
    for head in range(4):
        q = query_ref[:, head * HD : (head + 1) * HD]
        mix = jnp.zeros((rows, HD), F32)
        total = jnp.zeros((rows, 128), F32)
        for j in range(8):
            px = jnp.bitwise_xor(x, j % 4)
            pc = jnp.bitwise_xor(c, j // 4)
            pos = (base + (pc * 256 + px * 32)).astype(F32)
            s = lax.dot_general(q, slabs[j][:, :HD], NT, preferred_element_type=F32)
            w = jnp.where(pos < limit, jnp.exp(s), 0.0)
            total = total + (w[:, :128] + w[:, 128:])
            mix = mix + jnp.dot(w.astype(BF16), slabs[j][:, HD:], preferred_element_type=F32)
        total = jnp.sum(total, axis=-1, keepdims=True)
        total = jnp.where(total > 0.0, total, 1.0)
        out_ref[:, head * HD : (head + 1) * HD] = (mix / total).astype(BF16)


def limits(mib):
    return pltpu.CompilerParams(vmem_limit_bytes=mib << 20)


def gather_xc(piece):
    along_x = [piece] + [xor_permute(piece, "x", XS, k) for k in range(1, XS)]
    return along_x + [xor_permute(value, "c", CORES, 1) for value in along_x]


def gather_tensor(piece):
    return [piece] + [xor_permute(piece, ("y", "zl"), TENSOR, k) for k in range(1, TENSOR)]


def on_device(
    patches,
    enc_gain,
    enc_qkv,
    enc_out,
    cross_kv,
    key_gain,
    dec_hidden,
    dec_gain,
    query_weight,
    query_gain,
    image_of_row,
    valid_count,
):
    tensor_index = (lax.axis_index("y") * ZL + lax.axis_index("zl")).astype(jnp.int32)
    me = tensor_index.reshape(1)
    place = jnp.stack([lax.axis_index("zh"), lax.axis_index("x"), lax.axis_index("c")]).astype(
        jnp.int32
    )
    patch_rows, width = patches.shape
    rows = patch_rows * TENSOR
    own = image_permute(patches)

    dec_rows = dec_hidden.shape[0]
    dec_normed = rms_norm(dec_hidden.astype(F32), dec_gain).astype(BF16)
    queries = jnp.dot(dec_normed, query_weight, preferred_element_type=F32)
    queries = queries.reshape(dec_rows, -1, HD)
    queries = (rms_norm(queries, query_gain) / math.sqrt(HD)).astype(BF16)
    columns = jnp.stack([image_of_row, valid_count // 16, valid_count % 16], axis=1)
    message = jnp.concatenate(
        [
            queries.reshape(dec_rows, -1),
            jnp.pad(columns.astype(BF16), ((0, 0), (0, HD - 3))),
        ],
        axis=1,
    )

    pieces = gather_tensor(own)
    q, kv = pl.pallas_call(
        qkv_kernel,
        out_shape=(
            jax.ShapeDtypeStruct((2, rows, EHD), BF16),
            jax.ShapeDtypeStruct((4 * EHD, rows), BF16),
        ),
        in_specs=[smem()] + vmem(TENSOR + 2),
        out_specs=tuple(vmem(2)),
        scratch_shapes=[pltpu.VMEM((rows, width), BF16)],
        compiler_params=limits(12),
    )(me, *pieces, enc_gain.reshape(1, -1), enc_qkv.transpose(0, 2, 1))
    kv_pieces = gather_xc(kv)

    partial = pl.pallas_call(
        encoder_kernel,
        out_shape=jax.ShapeDtypeStruct((TENSOR, patch_rows, width), BF16),
        in_specs=vmem(10),
        out_specs=vmem(1)[0],
        scratch_shapes=[pltpu.VMEM((2, rows, 8 * rows), F32)],
        compiler_params=limits(20),
    )(q, *kv_pieces, enc_out)
    shares = lax.all_to_all(partial, ("y", "zl"), 0, 0)
    every_query = [message] + [xor_permute(message, "zh", ZH, k) for k in range(1, ZH)]
    encoded = (own.astype(F32) + jnp.sum(shares.astype(F32), axis=0)).astype(BF16)
    encoded_pieces = gather_tensor(encoded)
    slab = pl.pallas_call(
        cross_kernel,
        out_shape=jax.ShapeDtypeStruct((rows, 2 * HD), BF16),
        in_specs=[smem()] + vmem(TENSOR + 2),
        out_specs=vmem(1)[0],
        scratch_shapes=[pltpu.VMEM((rows, width), BF16)],
        compiler_params=limits(12),
    )(me, *encoded_pieces, cross_kv, key_gain.reshape(1, -1))
    slabs = gather_xc(slab)
    result = None
    for k in (2, 1, 3, 0):
        out = pl.pallas_call(
            decode_kernel,
            out_shape=jax.ShapeDtypeStruct((dec_rows, 4 * HD), BF16),
            in_specs=[smem()] + vmem(9),
            out_specs=vmem(1)[0],
            compiler_params=limits(12),
        )(place, every_query[k], *slabs)
        if k:
            out = xor_permute(out, "zh", ZH, k)
        result = out if result is None else result + out
    return result


def solution(mesh):
    parts = Mesh(mesh.devices.reshape(ZH, CORES, YS, ZL, XS), ("zh", "c", "y", "zl", "x"))
    group, tensor, seq = ("zh", "c"), ("y", "zl"), ("x",)
    in_specs = (
        P(group + tensor + seq, None),
        P(),
        P(None, None, tensor),
        P(tensor, None),
        P(None, tensor),
        P(),
        P(group + seq, None),
        P(),
        P(None, tensor),
        P(),
        P(group + seq),
        P(group + seq),
    )
    out_specs = P(group + seq, tensor)

    return jax.shard_map(
        on_device, mesh=parts, in_specs=in_specs, out_specs=out_specs, check_vma=False
    )
```

```python
import math

import jax
import jax.numpy as jnp
from jax import lax
from jax.experimental import pallas as pl
from jax.experimental.pallas import tpu as pltpu
from jax.sharding import Mesh
from jax.sharding import PartitionSpec as P

EHD = 80
HD = 128
EPSILON = 1e-05
F32 = jnp.float32
BF16 = jnp.bfloat16
ZH, CORES, YS, ZL, XS = 4, 2, 4, 2, 4
SHARE, SLOT = 20, 32
TENSOR = YS * ZL
NT = (((1,), (1,)), ((), ()))


def vmem(count):
    return [pl.BlockSpec(memory_space=pltpu.VMEM)] * count


def smem():
    return pl.BlockSpec(memory_space=pltpu.SMEM)


def xor_permute(values, axes, size, step):
    return lax.ppermute(values, axes, [(i, i ^ step) for i in range(size)])


def image_permute(values):
    pairs = []
    for zh in range(ZH):
        for y in range(YS):
            for zl in range(ZL):
                image, slot = (y % 2) * 2 + zl, zh * 2 + y // 2
                pairs.append(((zh * YS + y) * ZL + zl, image * TENSOR + slot))
    return lax.ppermute(values, ("zh", "y", "zl"), pairs)


def qkv_kernel(me_ref, *refs):
    pieces, refs = refs[:TENSOR], refs[TENSOR:]
    gain_ref, weight_ref, cross_ref, q_ref, kv_ref, fold_ref, base_ref, normed, raw, out_rows = refs
    me = me_ref[0]
    rows = raw.shape[0] // TENSOR
    for step in range(TENSOR):
        piece = pieces[step][:rows, :]
        values = piece.astype(F32)
        mean_value = jnp.mean(values, axis=-1, keepdims=True)
        centered = values - mean_value
        variance = jnp.mean(centered * centered, axis=-1, keepdims=True)
        result = centered * lax.rsqrt(variance + EPSILON) * gain_ref[...]
        place = pl.ds(pl.multiple_of(jnp.bitwise_xor(me, step) * rows, rows), rows)
        normed[place, :] = result.astype(BF16)
        raw[place, :] = piece
        share = pieces[step][rows:, :]
        fill = jnp.zeros((SLOT - share.shape[0], share.shape[1]), BF16)
        place = pl.ds(pl.multiple_of(jnp.bitwise_xor(me, step) * SLOT, SLOT), SLOT)
        out_rows[place, :] = jnp.concatenate([share, fill], axis=0)
    x = normed[...]
    width = 2 * EHD
    for part in range(2):
        out = lax.dot_general(weight_ref[1 + part], x, NT, preferred_element_type=F32)
        kv_ref[part * width : (part + 1) * width, :] = out.astype(BF16)
    q = lax.dot_general(x, weight_ref[0], NT, preferred_element_type=F32)
    for head in range(2):
        q_ref[head] = q[:, head * EHD : (head + 1) * EHD].astype(BF16)
    cross = cross_ref[...]
    fold_ref[...] = jnp.dot(out_rows[...], cross, preferred_element_type=F32).astype(BF16)
    base_ref[...] = jnp.dot(raw[...], cross, preferred_element_type=F32)


def encoder_kernel(q_ref, *refs):
    count = 8
    pieces, (out_ref, scores) = refs[:count], refs[count:]
    rows = q_ref.shape[1]
    scale = 1.0 / math.sqrt(EHD)
    spread = jnp.zeros(out_ref.shape, F32)
    for head in range(2):
        q = q_ref[head]
        top = None
        for j in range(count):
            s = jnp.dot(q, pieces[j][head * EHD : (head + 1) * EHD, :], preferred_element_type=F32)
            scores[head, :, j * rows : (j + 1) * rows] = s
            part = jnp.maximum(s[:, :128], s[:, 128:])
            top = part if top is None else jnp.maximum(top, part)
        top = jnp.max(top, axis=-1, keepdims=True)
        mix = jnp.zeros((rows, EHD), F32)
        total = jnp.zeros((rows, 128), F32)
        low = 2 * EHD + head * EHD
        for j in range(count):
            p = jnp.exp((scores[head, :, j * rows : (j + 1) * rows] - top) * scale)
            total = total + (p[:, :128] + p[:, 128:])
            mix = mix + lax.dot_general(
                p.astype(BF16), pieces[j][low : low + EHD, :], NT, preferred_element_type=F32
            )
        attended = (mix / jnp.sum(total, axis=-1, keepdims=True)).astype(BF16)
        feature = lax.broadcasted_iota(jnp.int32, (EHD, out_ref.shape[1]), 0) + head * EHD
        column = lax.broadcasted_iota(jnp.int32, (EHD, out_ref.shape[1]), 1)
        block = (feature * 3277) >> 16
        chosen = (column == feature + block * (SLOT - SHARE)).astype(F32).astype(BF16)
        spread = spread + jnp.dot(attended, chosen, preferred_element_type=F32)
    out_ref[...] = spread.astype(BF16)


def cross_kernel(me_ref, place_ref, *refs):
    pieces, folds, refs = refs[:TENSOR], refs[TENSOR : TENSOR + 8], refs[TENSOR + 8 :]
    base_ref, gain_ref, out_ref, weight = refs
    me, x, c = me_ref[0], place_ref[1], place_ref[2]
    size = 8 * SLOT
    for k in range(8):
        owner = jnp.bitwise_xor(c, k // 4) * 4 + jnp.bitwise_xor(x, k % 4)
        for t in range(TENSOR):
            low = pl.multiple_of(t * size + owner * SLOT, SLOT)
            weight[pl.ds(low, SLOT), :] = folds[k][t * SLOT : (t + 1) * SLOT, :]
    proj = base_ref[...]
    for step in range(TENSOR):
        low = pl.multiple_of(jnp.bitwise_xor(me, step) * size, size)
        proj = proj + jnp.dot(
            pieces[step][...], weight[pl.ds(low, size), :], preferred_element_type=F32
        )
    keys = proj[:, :HD]
    square_mean = jnp.mean(keys * keys, axis=-1, keepdims=True)
    keys = keys * lax.rsqrt(square_mean + EPSILON) * gain_ref[...]
    out_ref[:, :HD] = keys.astype(BF16)
    out_ref[:, HD:] = proj[:, HD:].astype(BF16)


def query_kernel(x_ref, gain_ref, weight_ref, head_gain_ref, image_ref, count_ref, out_ref, total, inverse):
    step = pl.program_id(0)
    rows = x_ref.shape[0]
    depth = weight_ref.shape[0]

    @pl.when(step == 0)
    def _():
        square = jnp.zeros((rows, 128), F32)
        for low in range(0, x_ref.shape[1], 128):
            part = x_ref[:, low : low + 128].astype(F32)
            square = square + part * part
        mean = jnp.sum(square, axis=-1, keepdims=True) / x_ref.shape[1]
        inverse[...] = jnp.broadcast_to(lax.rsqrt(mean + EPSILON), inverse.shape)
        total[...] = jnp.zeros_like(total)

    columns = pl.ds(pl.multiple_of(step * depth, depth), depth)
    normed = x_ref[:, columns].astype(F32) * inverse[:, 0:1] * gain_ref[:, columns]
    total[...] += jnp.dot(normed.astype(BF16), weight_ref[...], preferred_element_type=F32)

    @pl.when(step == pl.num_programs(0) - 1)
    def _():
        for head in range(4):
            q = total[:, head * HD : (head + 1) * HD]
            mean = jnp.mean(q * q, axis=-1, keepdims=True)
            q = q * lax.rsqrt(mean + EPSILON) * head_gain_ref[...] / math.sqrt(HD)
            out_ref[:rows, head * HD : (head + 1) * HD] = q.astype(BF16)
        count = count_ref[...]
        extra = jnp.concatenate([image_ref[...], count >> 4, count & 15], axis=0)
        extra = jnp.concatenate([extra, jnp.zeros((13, rows), jnp.int32)], axis=0)
        out_ref[rows:, :rows] = extra.astype(F32).astype(BF16)
        out_ref[rows:, rows:] = jnp.zeros((16, out_ref.shape[1] - rows), BF16)


def decode_kernel(place_ref, query_ref, *refs):
    slabs, out_ref = refs[:8], refs[8]
    keys = slabs[0].shape[0]
    zh, x, c = place_ref[0], place_ref[1], place_ref[2]
    lane = lax.broadcasted_iota(jnp.int32, (1, keys), 1)
    base = (lane >> 6) * 512 + ((lane >> 5) & 1) * 128 + (lane & 31)
    rows = out_ref.shape[0]
    extra = query_ref[rows : rows + 8, :HD].astype(F32)
    limit = jnp.where(extra[0:1] == zh.astype(F32), extra[1:2] * 16.0 + extra[2:3], 0.0)
    limit = jnp.broadcast_to(limit, (8, rows)).T[:, 0:1]
    for head in range(4):
        q = query_ref[:rows, head * HD : (head + 1) * HD]
        mix = jnp.zeros((rows, HD), F32)
        total = jnp.zeros((rows, 128), F32)
        for j in range(8):
            px = jnp.bitwise_xor(x, j % 4)
            pc = jnp.bitwise_xor(c, j // 4)
            pos = (base + (pc * 256 + px * 32)).astype(F32)
            s = lax.dot_general(q, slabs[j][:, :HD], NT, preferred_element_type=F32)
            w = jnp.where(pos < limit, jnp.exp(s), 0.0)
            total = total + (w[:, :128] + w[:, 128:])
            mix = mix + jnp.dot(w.astype(BF16), slabs[j][:, HD:], preferred_element_type=F32)
        total = jnp.sum(total, axis=-1, keepdims=True)
        total = jnp.where(total > 0.0, total, 1.0)
        out_ref[:, head * HD : (head + 1) * HD] = (mix / total).astype(BF16)


def limits(mib):
    return pltpu.CompilerParams(vmem_limit_bytes=mib << 20)


def gather_xc(piece):
    along_x = [piece] + [xor_permute(piece, "x", XS, k) for k in range(1, XS)]
    return along_x + [xor_permute(value, "c", CORES, 1) for value in along_x]


def gather_tensor(piece):
    pieces = {0: piece}
    for k in (5, 7, 3, 4, 6, 2, 1):
        pieces[k] = xor_permute(piece, ("y", "zl"), TENSOR, k)
    return [pieces[k] for k in range(TENSOR)]


def on_device(
    patches,
    enc_gain,
    enc_qkv,
    enc_out,
    cross_kv,
    key_gain,
    dec_hidden,
    dec_gain,
    query_weight,
    query_gain,
    image_of_row,
    valid_count,
):
    tensor_index = (lax.axis_index("y") * ZL + lax.axis_index("zl")).astype(jnp.int32)
    me = tensor_index.reshape(1)
    place = jnp.stack([lax.axis_index("zh"), lax.axis_index("x"), lax.axis_index("c")]).astype(
        jnp.int32
    )
    patch_rows, width = patches.shape
    rows = patch_rows * TENSOR
    own = image_permute(patches)

    dec_rows = dec_hidden.shape[0]
    depth = 1024
    query_width = query_weight.shape[1]
    message = pl.pallas_call(
        query_kernel,
        grid=(dec_hidden.shape[1] // depth,),
        out_shape=jax.ShapeDtypeStruct((dec_rows + 16, query_width), BF16),
        in_specs=[
            pl.BlockSpec(dec_hidden.shape, lambda i: (0, 0)),
            pl.BlockSpec((1, dec_hidden.shape[1]), lambda i: (0, 0)),
            pl.BlockSpec((depth, query_width), lambda i: (i, 0)),
            pl.BlockSpec((1, HD), lambda i: (0, 0)),
            pl.BlockSpec((1, dec_rows), lambda i: (0, 0)),
            pl.BlockSpec((1, dec_rows), lambda i: (0, 0)),
        ],
        out_specs=pl.BlockSpec((dec_rows + 16, query_width), lambda i: (0, 0)),
        scratch_shapes=[pltpu.VMEM((dec_rows, query_width), F32), pltpu.VMEM((dec_rows, 128), F32)],
        compiler_params=limits(56),
    )(
        dec_hidden,
        dec_gain.reshape(1, -1),
        query_weight,
        query_gain.reshape(1, -1),
        image_of_row.reshape(1, -1),
        valid_count.reshape(1, -1),
    )

    owner = lax.axis_index("c") * XS + lax.axis_index("x")
    share = lax.dynamic_slice_in_dim(enc_out, owner * SHARE, SHARE, axis=0)
    share = jnp.pad(share, ((0, 24 - SHARE), (0, 0)))
    pieces = gather_tensor(jnp.concatenate([own, share], axis=0))
    q, kv, fold, base = pl.pallas_call(
        qkv_kernel,
        out_shape=(
            jax.ShapeDtypeStruct((2, rows, EHD), BF16),
            jax.ShapeDtypeStruct((4 * EHD, rows), BF16),
            jax.ShapeDtypeStruct((TENSOR * SLOT, 2 * HD), BF16),
            jax.ShapeDtypeStruct((rows, 2 * HD), F32),
        ),
        in_specs=[smem()] + vmem(TENSOR + 3),
        out_specs=tuple(vmem(4)),
        scratch_shapes=[
            pltpu.VMEM((rows, width), BF16),
            pltpu.VMEM((rows, width), BF16),
            pltpu.VMEM((TENSOR * SLOT, width), BF16),
        ],
        compiler_params=limits(16),
    )(me, *pieces, enc_gain.reshape(1, -1), enc_qkv.transpose(0, 2, 1), cross_kv)
    kv_pieces = gather_xc(kv)
    every_query = [message] + [xor_permute(message, "zh", ZH, k) for k in range(1, ZH)]

    attended = pl.pallas_call(
        encoder_kernel,
        out_shape=jax.ShapeDtypeStruct((rows, 8 * SLOT), BF16),
        in_specs=vmem(9),
        out_specs=vmem(1)[0],
        scratch_shapes=[pltpu.VMEM((2, rows, 8 * rows), F32)],
        compiler_params=limits(20),
    )(q, *kv_pieces)
    attended_pieces = gather_tensor(attended)
    folds = gather_xc(fold)
    slab = pl.pallas_call(
        cross_kernel,
        out_shape=jax.ShapeDtypeStruct((rows, 2 * HD), BF16),
        in_specs=[smem()] * 2 + vmem(TENSOR + 10),
        out_specs=vmem(1)[0],
        scratch_shapes=[pltpu.VMEM((TENSOR * 8 * SLOT, 2 * HD), BF16)],
        compiler_params=limits(12),
    )(me, place, *attended_pieces, *folds, base, key_gain.reshape(1, -1))
    slabs = gather_xc(slab)
    result = None
    for k in (2, 1, 3, 0):
        out = pl.pallas_call(
            decode_kernel,
            out_shape=jax.ShapeDtypeStruct((dec_rows, 4 * HD), BF16),
            in_specs=[smem()] + vmem(9),
            out_specs=vmem(1)[0],
            compiler_params=limits(12),
        )(place, every_query[k], *slabs)
        if k:
            out = xor_permute(out, "zh", ZH, k)
        result = out if result is None else result + out
    return result


def solution(mesh):
    parts = Mesh(mesh.devices.reshape(ZH, CORES, YS, ZL, XS), ("zh", "c", "y", "zl", "x"))
    group, tensor, seq = ("zh", "c"), ("y", "zl"), ("x",)
    in_specs = (
        P(group + tensor + seq, None),
        P(),
        P(None, None, tensor),
        P(tensor, None),
        P(None, tensor),
        P(),
        P(group + seq, None),
        P(),
        P(None, tensor),
        P(),
        P(group + seq),
        P(group + seq),
    )
    out_specs = P(group + seq, tensor)

    return jax.shard_map(
        on_device, mesh=parts, in_specs=in_specs, out_specs=out_specs, check_vma=False
    )
```

```python
import math

import jax
import jax.numpy as jnp
from jax import lax
from jax.experimental import pallas as pl
from jax.experimental.pallas import tpu as pltpu
from jax.sharding import Mesh
from jax.sharding import PartitionSpec as P

EHD = 80
HD = 128
EPSILON = 1e-05
F32 = jnp.float32
BF16 = jnp.bfloat16
ZH, CORES, YS, ZL, XS = 4, 2, 4, 2, 4
SHARE, SLOT = 20, 32
TENSOR = YS * ZL
NT = (((1,), (1,)), ((), ()))


def vmem(count):
    return [pl.BlockSpec(memory_space=pltpu.VMEM)] * count


def smem():
    return pl.BlockSpec(memory_space=pltpu.SMEM)


def xor_permute(values, axes, size, step):
    return lax.ppermute(values, axes, [(i, i ^ step) for i in range(size)])


def image_permute(values):
    pairs = []
    for zh in range(ZH):
        for y in range(YS):
            for zl in range(ZL):
                image, slot = (y % 2) * 2 + zl, zh * 2 + y // 2
                pairs.append(((zh * YS + y) * ZL + zl, image * TENSOR + slot))
    return lax.ppermute(values, ("zh", "y", "zl"), pairs)


def qkv_kernel(me_ref, *refs):
    pieces, refs = refs[:TENSOR], refs[TENSOR:]
    gain_ref, weight_ref, cross_ref, q_ref, kv_ref, base_ref, normed, raw, out_rows = refs
    me = me_ref[0]
    rows = raw.shape[0] // TENSOR
    for step in range(TENSOR):
        piece = pieces[step][:rows, :]
        values = piece.astype(F32)
        mean_value = jnp.mean(values, axis=-1, keepdims=True)
        centered = values - mean_value
        variance = jnp.mean(centered * centered, axis=-1, keepdims=True)
        result = centered * lax.rsqrt(variance + EPSILON) * gain_ref[...]
        place = pl.ds(pl.multiple_of(jnp.bitwise_xor(me, step) * rows, rows), rows)
        normed[place, :] = result.astype(BF16)
        raw[place, :] = piece
        share = pieces[step][rows:, :]
        fill = jnp.zeros((SLOT - share.shape[0], share.shape[1]), BF16)
        place = pl.ds(pl.multiple_of(jnp.bitwise_xor(me, step) * SLOT, SLOT), SLOT)
        out_rows[place, :] = jnp.concatenate([share, fill], axis=0)
    x = normed[...]
    width = 2 * EHD
    for part in range(2):
        out = lax.dot_general(weight_ref[1 + part], x, NT, preferred_element_type=F32)
        kv_ref[part * width : (part + 1) * width, :] = out.astype(BF16)
    q = lax.dot_general(x, weight_ref[0], NT, preferred_element_type=F32)
    for head in range(2):
        q_ref[head] = q[:, head * EHD : (head + 1) * EHD].astype(BF16)
    cross = cross_ref[...]
    fold = jnp.dot(out_rows[...], cross, preferred_element_type=F32)
    kv_ref[4 * EHD :, :] = fold.astype(BF16)
    base_ref[...] = jnp.dot(raw[...], cross, preferred_element_type=F32)


def encoder_kernel(q_ref, *refs):
    count = 8
    pieces, (out_ref, scores) = refs[:count], refs[count:]
    rows = q_ref.shape[1]
    scale = 1.0 / math.sqrt(EHD)
    spread = jnp.zeros(out_ref.shape, F32)
    for head in range(2):
        q = q_ref[head]
        top = None
        for j in range(count):
            s = jnp.dot(q, pieces[j][head * EHD : (head + 1) * EHD, :], preferred_element_type=F32)
            scores[head, :, j * rows : (j + 1) * rows] = s
            part = jnp.maximum(s[:, :128], s[:, 128:])
            top = part if top is None else jnp.maximum(top, part)
        top = jnp.max(top, axis=-1, keepdims=True)
        mix = jnp.zeros((rows, EHD), F32)
        total = jnp.zeros((rows, 128), F32)
        low = 2 * EHD + head * EHD
        for j in range(count):
            p = jnp.exp((scores[head, :, j * rows : (j + 1) * rows] - top) * scale)
            total = total + (p[:, :128] + p[:, 128:])
            mix = mix + lax.dot_general(
                p.astype(BF16), pieces[j][low : low + EHD, :], NT, preferred_element_type=F32
            )
        attended = (mix / jnp.sum(total, axis=-1, keepdims=True)).astype(BF16)
        feature = lax.broadcasted_iota(jnp.int32, (EHD, out_ref.shape[1]), 0) + head * EHD
        column = lax.broadcasted_iota(jnp.int32, (EHD, out_ref.shape[1]), 1)
        block = (feature * 3277) >> 16
        chosen = (column == feature + block * (SLOT - SHARE)).astype(F32).astype(BF16)
        spread = spread + jnp.dot(attended, chosen, preferred_element_type=F32)
    out_ref[...] = spread.astype(BF16)


def cross_kernel(me_ref, place_ref, *refs):
    pieces, folds, refs = refs[:TENSOR], refs[TENSOR : TENSOR + 8], refs[TENSOR + 8 :]
    base_ref, gain_ref, out_ref, weight = refs
    me, x, c = me_ref[0], place_ref[1], place_ref[2]
    size = 8 * SLOT
    for k in range(8):
        owner = jnp.bitwise_xor(c, k // 4) * 4 + jnp.bitwise_xor(x, k % 4)
        for t in range(TENSOR):
            low = pl.multiple_of(t * size + owner * SLOT, SLOT)
            first = 4 * EHD + t * SLOT
            weight[pl.ds(low, SLOT), :] = folds[k][first : first + SLOT, :]
    proj = base_ref[...]
    for step in range(TENSOR):
        low = pl.multiple_of(jnp.bitwise_xor(me, step) * size, size)
        proj = proj + jnp.dot(
            pieces[step][...], weight[pl.ds(low, size), :], preferred_element_type=F32
        )
    keys = proj[:, :HD]
    square_mean = jnp.mean(keys * keys, axis=-1, keepdims=True)
    keys = keys * lax.rsqrt(square_mean + EPSILON) * gain_ref[...]
    out_ref[:, :HD] = keys.astype(BF16)
    out_ref[:, HD:] = proj[:, HD:].astype(BF16)


def query_part(x_ref, gain_ref, weight_ref, total, inverse):
    depth = weight_ref.shape[0]
    columns = pl.ds(pl.multiple_of(pl.program_id(0) * depth, depth), depth)
    normed = x_ref[:, columns].astype(F32) * inverse[:, 0:1] * gain_ref[:, columns]
    total[...] += jnp.dot(normed.astype(BF16), weight_ref[...], preferred_element_type=F32)


def query_first_kernel(x_ref, gain_ref, weight_ref, total, inverse):
    @pl.when(pl.program_id(0) == 0)
    def _():
        square = jnp.zeros((x_ref.shape[0], 128), F32)
        for low in range(0, x_ref.shape[1], 128):
            part = x_ref[:, low : low + 128].astype(F32)
            square = square + part * part
        mean = jnp.sum(square, axis=-1, keepdims=True) / x_ref.shape[1]
        inverse[...] = jnp.broadcast_to(lax.rsqrt(mean + EPSILON), inverse.shape)
        total[...] = jnp.zeros_like(total)

    query_part(x_ref, gain_ref, weight_ref, total, inverse)


def query_last_kernel(
    x_ref, gain_ref, weight_ref, begun, inverse, head_gain_ref, image_ref, count_ref, out_ref, total
):
    rows = x_ref.shape[0]

    @pl.when(pl.program_id(0) == 0)
    def _():
        total[...] = begun[...]

    query_part(x_ref, gain_ref, weight_ref, total, inverse)

    @pl.when(pl.program_id(0) == pl.num_programs(0) - 1)
    def _():
        for head in range(4):
            q = total[:, head * HD : (head + 1) * HD]
            mean = jnp.mean(q * q, axis=-1, keepdims=True)
            q = q * lax.rsqrt(mean + EPSILON) * head_gain_ref[...] / math.sqrt(HD)
            out_ref[:rows, head * HD : (head + 1) * HD] = q.astype(BF16)
        count = count_ref[...]
        extra = jnp.concatenate([image_ref[...], count >> 4, count & 15], axis=0)
        extra = jnp.concatenate([extra, jnp.zeros((13, rows), jnp.int32)], axis=0)
        out_ref[rows:, :rows] = extra.astype(F32).astype(BF16)
        out_ref[rows:, rows:] = jnp.zeros((16, out_ref.shape[1] - rows), BF16)


def decode_kernel(place_ref, query_ref, *refs):
    slabs, out_ref = refs[:8], refs[8]
    keys = slabs[0].shape[0]
    zh, x, c = place_ref[0], place_ref[1], place_ref[2]
    lane = lax.broadcasted_iota(jnp.int32, (1, keys), 1)
    base = (lane >> 6) * 512 + ((lane >> 5) & 1) * 128 + (lane & 31)
    rows = out_ref.shape[0]
    extra = query_ref[rows : rows + 8, :HD].astype(F32)
    limit = jnp.where(extra[0:1] == zh.astype(F32), extra[1:2] * 16.0 + extra[2:3], 0.0)
    limit = jnp.broadcast_to(limit, (8, rows)).T[:, 0:1]
    for head in range(4):
        q = query_ref[:rows, head * HD : (head + 1) * HD]
        mix = jnp.zeros((rows, HD), F32)
        total = jnp.zeros((rows, 128), F32)
        for j in range(8):
            px = jnp.bitwise_xor(x, j % 4)
            pc = jnp.bitwise_xor(c, j // 4)
            pos = (base + (pc * 256 + px * 32)).astype(F32)
            s = lax.dot_general(q, slabs[j][:, :HD], NT, preferred_element_type=F32)
            w = jnp.where(pos < limit, jnp.exp(s), 0.0)
            total = total + (w[:, :128] + w[:, 128:])
            mix = mix + jnp.dot(w.astype(BF16), slabs[j][:, HD:], preferred_element_type=F32)
        total = jnp.sum(total, axis=-1, keepdims=True)
        total = jnp.where(total > 0.0, total, 1.0)
        out_ref[:, head * HD : (head + 1) * HD] = (mix / total).astype(BF16)


def limits(mib):
    return pltpu.CompilerParams(vmem_limit_bytes=mib << 20)


def gather_xc(piece):
    along_x = [piece] + [xor_permute(piece, "x", XS, k) for k in range(1, XS)]
    return along_x + [xor_permute(value, "c", CORES, 1) for value in along_x]


def gather_tensor(piece):
    pieces = {0: piece}
    for k in (5, 7, 3, 4, 6, 2, 1):
        pieces[k] = xor_permute(piece, ("y", "zl"), TENSOR, k)
    return [pieces[k] for k in range(TENSOR)]


def on_device(
    patches,
    enc_gain,
    enc_qkv,
    enc_out,
    cross_kv,
    key_gain,
    dec_hidden,
    dec_gain,
    query_weight,
    query_gain,
    image_of_row,
    valid_count,
):
    tensor_index = (lax.axis_index("y") * ZL + lax.axis_index("zl")).astype(jnp.int32)
    me = tensor_index.reshape(1)
    place = jnp.stack([lax.axis_index("zh"), lax.axis_index("x"), lax.axis_index("c")]).astype(
        jnp.int32
    )
    patch_rows, width = patches.shape
    rows = patch_rows * TENSOR
    own = image_permute(patches)

    dec_rows = dec_hidden.shape[0]
    depth, steps = 1024, 4
    dec_width, query_width = query_weight.shape
    fixed = lambda shape: pl.BlockSpec(shape, lambda i: (0, 0))
    gain_view = dec_gain.reshape(1, -1)
    begun, inverse = pl.pallas_call(
        query_first_kernel,
        grid=(steps,),
        out_shape=(
            jax.ShapeDtypeStruct((dec_rows, query_width), F32),
            jax.ShapeDtypeStruct((dec_rows, 128), F32),
        ),
        in_specs=[
            fixed((dec_rows, dec_width)),
            fixed((1, dec_width)),
            pl.BlockSpec((depth, query_width), lambda i: (i, 0)),
        ],
        out_specs=(fixed((dec_rows, query_width)), fixed((dec_rows, 128))),
        compiler_params=limits(56),
    )(dec_hidden, gain_view, query_weight)
    message = pl.pallas_call(
        query_last_kernel,
        grid=(steps,),
        out_shape=jax.ShapeDtypeStruct((dec_rows + 16, query_width), BF16),
        in_specs=[
            pl.BlockSpec((dec_rows, dec_width // 2), lambda i: (0, 1)),
            pl.BlockSpec((1, dec_width // 2), lambda i: (0, 1)),
            pl.BlockSpec((depth, query_width), lambda i: (i + steps, 0)),
            fixed((dec_rows, query_width)),
            fixed((dec_rows, 128)),
            fixed((1, HD)),
            fixed((1, dec_rows)),
            fixed((1, dec_rows)),
        ],
        out_specs=fixed((dec_rows + 16, query_width)),
        scratch_shapes=[pltpu.VMEM((dec_rows, query_width), F32)],
        compiler_params=limits(56),
    )(
        dec_hidden,
        gain_view,
        query_weight,
        begun,
        inverse,
        query_gain.reshape(1, -1),
        image_of_row.reshape(1, -1),
        valid_count.reshape(1, -1),
    )

    owner = lax.axis_index("c") * XS + lax.axis_index("x")
    share = lax.dynamic_slice_in_dim(enc_out, owner * SHARE, SHARE, axis=0)
    share = jnp.pad(share, ((0, 24 - SHARE), (0, 0)))
    gain_row = enc_gain.reshape(1, -1)
    pieces = gather_tensor(jnp.concatenate([own, share], axis=0))
    q, kv, base = pl.pallas_call(
        qkv_kernel,
        out_shape=(
            jax.ShapeDtypeStruct((2, rows, EHD), BF16),
            jax.ShapeDtypeStruct((4 * EHD + TENSOR * SLOT, rows), BF16),
            jax.ShapeDtypeStruct((rows, 2 * HD), F32),
        ),
        in_specs=[smem()] + vmem(TENSOR + 3),
        out_specs=tuple(vmem(3)),
        scratch_shapes=[
            pltpu.VMEM((rows, width), BF16),
            pltpu.VMEM((rows, width), BF16),
            pltpu.VMEM((TENSOR * SLOT, width), BF16),
        ],
        compiler_params=limits(16),
    )(me, *pieces, gain_row, enc_qkv.transpose(0, 2, 1), cross_kv)
    kv_pieces = gather_xc(kv)
    every_query = [message] + [xor_permute(message, "zh", ZH, k) for k in range(1, ZH)]

    attended = pl.pallas_call(
        encoder_kernel,
        out_shape=jax.ShapeDtypeStruct((rows, 8 * SLOT), BF16),
        in_specs=vmem(9),
        out_specs=vmem(1)[0],
        scratch_shapes=[pltpu.VMEM((2, rows, 8 * rows), F32)],
        compiler_params=limits(20),
    )(q, *kv_pieces)
    attended_pieces = gather_tensor(attended)
    slab = pl.pallas_call(
        cross_kernel,
        out_shape=jax.ShapeDtypeStruct((rows, 2 * HD), BF16),
        in_specs=[smem()] * 2 + vmem(TENSOR + 10),
        out_specs=vmem(1)[0],
        scratch_shapes=[pltpu.VMEM((TENSOR * 8 * SLOT, 2 * HD), BF16)],
        compiler_params=limits(12),
    )(me, place, *attended_pieces, *kv_pieces, base, key_gain.reshape(1, -1))
    slabs = gather_xc(slab)
    result = None
    for k in (2, 1, 3, 0):
        out = pl.pallas_call(
            decode_kernel,
            out_shape=jax.ShapeDtypeStruct((dec_rows, 4 * HD), BF16),
            in_specs=[smem()] + vmem(9),
            out_specs=vmem(1)[0],
            compiler_params=limits(12),
        )(place, every_query[k], *slabs)
        if k:
            out = xor_permute(out, "zh", ZH, k)
        result = out if result is None else result + out
    return result


def solution(mesh):
    parts = Mesh(mesh.devices.reshape(ZH, CORES, YS, ZL, XS), ("zh", "c", "y", "zl", "x"))
    group, tensor, seq = ("zh", "c"), ("y", "zl"), ("x",)
    in_specs = (
        P(group + tensor + seq, None),
        P(),
        P(None, None, tensor),
        P(tensor, None),
        P(None, tensor),
        P(),
        P(group + seq, None),
        P(),
        P(None, tensor),
        P(),
        P(group + seq),
        P(group + seq),
    )
    out_specs = P(group + seq, tensor)

    return jax.shard_map(
        on_device, mesh=parts, in_specs=in_specs, out_specs=out_specs, check_vma=False
    )
```

```python
import math

import jax
import jax.numpy as jnp
from jax import lax
from jax.experimental import pallas as pl
from jax.experimental.pallas import tpu as pltpu
from jax.sharding import Mesh
from jax.sharding import PartitionSpec as P

EHD = 80
HD = 128
EPSILON = 1e-05
F32 = jnp.float32
BF16 = jnp.bfloat16
ZH, CORES, YS, ZL, XS = 4, 2, 4, 2, 4
SHARE, SLOT = 20, 32
TENSOR = YS * ZL
NT = (((1,), (1,)), ((), ()))


def vmem(count):
    return [pl.BlockSpec(memory_space=pltpu.VMEM)] * count


def smem():
    return pl.BlockSpec(memory_space=pltpu.SMEM)


def xor_permute(values, axes, size, step):
    return lax.ppermute(values, axes, [(i, i ^ step) for i in range(size)])


def image_permute(values):
    pairs = []
    for zh in range(ZH):
        for y in range(YS):
            for zl in range(ZL):
                image, slot = (y % 2) * 2 + zl, zh * 2 + y // 2
                pairs.append(((zh * YS + y) * ZL + zl, image * TENSOR + slot))
    return lax.ppermute(values, ("zh", "y", "zl"), pairs)


def qkv_kernel(me_ref, *refs):
    pieces, refs = refs[:TENSOR], refs[TENSOR:]
    gain_ref, weight_ref, cross_ref, q_ref, kv_ref, base_ref, normed, raw, out_rows = refs
    me = me_ref[0]
    rows = raw.shape[0] // TENSOR
    for step in range(TENSOR):
        piece = pieces[step][:rows, :]
        values = piece.astype(F32)
        mean_value = jnp.mean(values, axis=-1, keepdims=True)
        centered = values - mean_value
        variance = jnp.mean(centered * centered, axis=-1, keepdims=True)
        result = centered * lax.rsqrt(variance + EPSILON) * gain_ref[...]
        place = pl.ds(pl.multiple_of(jnp.bitwise_xor(me, step) * rows, rows), rows)
        normed[place, :] = result.astype(BF16)
        raw[place, :] = piece
        share = pieces[step][rows:, :]
        fill = jnp.zeros((SLOT - share.shape[0], share.shape[1]), BF16)
        place = pl.ds(pl.multiple_of(jnp.bitwise_xor(me, step) * SLOT, SLOT), SLOT)
        out_rows[place, :] = jnp.concatenate([share, fill], axis=0)
    x = normed[...]
    width = 2 * EHD
    for part in range(2):
        out = lax.dot_general(weight_ref[1 + part], x, NT, preferred_element_type=F32)
        kv_ref[part * width : (part + 1) * width, :] = out.astype(BF16)
    q = lax.dot_general(x, weight_ref[0], NT, preferred_element_type=F32)
    for head in range(2):
        q_ref[head] = q[:, head * EHD : (head + 1) * EHD].astype(BF16)
    cross = cross_ref[...]
    fold = jnp.dot(out_rows[...], cross, preferred_element_type=F32)
    row = lax.broadcasted_iota(jnp.int32, (TENSOR * SHARE, TENSOR * SLOT), 0)
    column = lax.broadcasted_iota(jnp.int32, (TENSOR * SHARE, TENSOR * SLOT), 1)
    chosen = (column == row + ((row * 3277) >> 16) * (SLOT - SHARE)).astype(F32).astype(BF16)
    fold = jnp.dot(chosen, fold.astype(BF16), preferred_element_type=F32)
    kv_ref[4 * EHD :, :] = fold.astype(BF16)
    base_ref[...] = jnp.dot(raw[...], cross, preferred_element_type=F32)


def encoder_kernel(q_ref, *refs):
    count = 8
    pieces, (out_ref, scores) = refs[:count], refs[count:]
    rows = q_ref.shape[1]
    scale = 1.0 / math.sqrt(EHD)
    for head in range(2):
        q = q_ref[head]
        top = None
        for j in range(count):
            s = jnp.dot(q, pieces[j][head * EHD : (head + 1) * EHD, :], preferred_element_type=F32)
            scores[head, :, j * rows : (j + 1) * rows] = s
            part = jnp.maximum(s[:, :128], s[:, 128:])
            top = part if top is None else jnp.maximum(top, part)
        top = jnp.max(top, axis=-1, keepdims=True)
        mix = jnp.zeros((rows, EHD), F32)
        total = jnp.zeros((rows, 128), F32)
        low = 2 * EHD + head * EHD
        for j in range(count):
            p = jnp.exp((scores[head, :, j * rows : (j + 1) * rows] - top) * scale)
            total = total + (p[:, :128] + p[:, 128:])
            mix = mix + lax.dot_general(
                p.astype(BF16), pieces[j][low : low + EHD, :], NT, preferred_element_type=F32
            )
        attended = mix / jnp.sum(total, axis=-1, keepdims=True)
        out_ref[head * EHD : (head + 1) * EHD, :] = attended.T.astype(BF16)


def fold_kernel(place_ref, *refs):
    pieces, (out_ref, stacked) = refs[:8], refs[8:]
    x, c = place_ref[1], place_ref[2]
    size = TENSOR * SHARE
    for k in range(8):
        owner = jnp.bitwise_xor(c, k // 4) * 4 + jnp.bitwise_xor(x, k % 4)
        low = pl.multiple_of(owner * size, size)
        stacked[pl.ds(low, size), :] = pieces[k][4 * EHD :, :]
    for t in range(TENSOR):
        row = lax.broadcasted_iota(jnp.int32, (size, 8 * size), 0)
        column = lax.broadcasted_iota(jnp.int32, (size, 8 * size), 1)
        owner = (row * 3277) >> 16
        source = owner * (size - SHARE) + row + t * SHARE
        chosen = (column == source).astype(F32).astype(BF16)
        out = jnp.dot(chosen, stacked[...], preferred_element_type=F32)
        out_ref[t] = out.astype(BF16)


def cross_kernel(me_ref, *refs):
    pieces, (weight_ref, base_ref, gain_ref, out_ref) = refs[:TENSOR], refs[TENSOR:]
    me = me_ref[0]
    proj = base_ref[...]
    for step in range(TENSOR):
        weight = weight_ref[jnp.bitwise_xor(me, step)]
        proj = proj + lax.dot_general(
            pieces[step][...], weight, (((0,), (0,)), ((), ())), preferred_element_type=F32
        )
    keys = proj[:, :HD]
    square_mean = jnp.mean(keys * keys, axis=-1, keepdims=True)
    keys = keys * lax.rsqrt(square_mean + EPSILON) * gain_ref[...]
    out_ref[:, :HD] = keys.astype(BF16)
    out_ref[:, HD:] = proj[:, HD:].astype(BF16)


def query_part(x_ref, gain_ref, weight_ref, total, inverse):
    depth = weight_ref.shape[0]
    columns = pl.ds(pl.multiple_of(pl.program_id(0) * depth, depth), depth)
    normed = x_ref[:, columns].astype(F32) * inverse[:, 0:1] * gain_ref[:, columns]
    total[...] += jnp.dot(normed.astype(BF16), weight_ref[...], preferred_element_type=F32)


def query_first_kernel(x_ref, gain_ref, weight_ref, total, inverse):
    @pl.when(pl.program_id(0) == 0)
    def _():
        square = jnp.zeros((x_ref.shape[0], 128), F32)
        for low in range(0, x_ref.shape[1], 128):
            part = x_ref[:, low : low + 128].astype(F32)
            square = square + part * part
        mean = jnp.sum(square, axis=-1, keepdims=True) / x_ref.shape[1]
        inverse[...] = jnp.broadcast_to(lax.rsqrt(mean + EPSILON), inverse.shape)
        total[...] = jnp.zeros_like(total)

    query_part(x_ref, gain_ref, weight_ref, total, inverse)


def query_last_kernel(
    x_ref, gain_ref, weight_ref, begun, inverse, head_gain_ref, image_ref, count_ref, out_ref, total
):
    rows = x_ref.shape[0]

    @pl.when(pl.program_id(0) == 0)
    def _():
        total[...] = begun[...]

    query_part(x_ref, gain_ref, weight_ref, total, inverse)

    @pl.when(pl.program_id(0) == pl.num_programs(0) - 1)
    def _():
        for head in range(4):
            q = total[:, head * HD : (head + 1) * HD]
            mean = jnp.mean(q * q, axis=-1, keepdims=True)
            q = q * lax.rsqrt(mean + EPSILON) * head_gain_ref[...] / math.sqrt(HD)
            out_ref[:rows, head * HD : (head + 1) * HD] = q.astype(BF16)
        count = count_ref[...]
        extra = jnp.concatenate([image_ref[...], count >> 4, count & 15], axis=0)
        extra = jnp.concatenate([extra, jnp.zeros((13, rows), jnp.int32)], axis=0)
        out_ref[rows:, :rows] = extra.astype(F32).astype(BF16)
        out_ref[rows:, rows:] = jnp.zeros((16, out_ref.shape[1] - rows), BF16)


def decode_kernel(place_ref, query_ref, *refs):
    slabs, out_ref = refs[:8], refs[8]
    keys = slabs[0].shape[0]
    zh, x, c = place_ref[0], place_ref[1], place_ref[2]
    lane = lax.broadcasted_iota(jnp.int32, (1, keys), 1)
    base = (lane >> 6) * 512 + ((lane >> 5) & 1) * 128 + (lane & 31)
    rows = out_ref.shape[0]
    extra = query_ref[rows : rows + 8, :HD].astype(F32)
    limit = jnp.where(extra[0:1] == zh.astype(F32), extra[1:2] * 16.0 + extra[2:3], 0.0)
    limit = jnp.broadcast_to(limit, (8, rows)).T[:, 0:1]
    limit = jnp.concatenate([limit] * 4, axis=0)
    q = [query_ref[:rows, head * HD : (head + 1) * HD] for head in range(4)]
    q = jnp.concatenate(q, axis=0)
    mix = jnp.zeros((4 * rows, HD), F32)
    total = jnp.zeros((4 * rows, 128), F32)
    for j in range(8):
        px = jnp.bitwise_xor(x, j % 4)
        pc = jnp.bitwise_xor(c, j // 4)
        pos = (base + (pc * 256 + px * 32)).astype(F32)
        s = lax.dot_general(q, slabs[j][:, :HD], NT, preferred_element_type=F32)
        w = jnp.where(pos < limit, jnp.exp(s), 0.0)
        total = total + (w[:, :128] + w[:, 128:])
        mix = mix + jnp.dot(w.astype(BF16), slabs[j][:, HD:], preferred_element_type=F32)
    total = jnp.sum(total, axis=-1, keepdims=True)
    mix = mix / jnp.where(total > 0.0, total, 1.0)
    for head in range(4):
        part = mix[head * rows : (head + 1) * rows]
        out_ref[:, head * HD : (head + 1) * HD] = part.astype(BF16)


def limits(mib):
    return pltpu.CompilerParams(vmem_limit_bytes=mib << 20)


def gather_xc(piece):
    along_x = [piece] + [xor_permute(piece, "x", XS, k) for k in range(1, XS)]
    return along_x + [xor_permute(value, "c", CORES, 1) for value in along_x]


def gather_tensor(piece):
    pieces = {0: piece}
    for k in (5, 7, 3, 4, 6, 2, 1):
        pieces[k] = xor_permute(piece, ("y", "zl"), TENSOR, k)
    return [pieces[k] for k in range(TENSOR)]


def on_device(
    patches,
    enc_gain,
    enc_qkv,
    enc_out,
    cross_kv,
    key_gain,
    dec_hidden,
    dec_gain,
    query_weight,
    query_gain,
    image_of_row,
    valid_count,
):
    tensor_index = (lax.axis_index("y") * ZL + lax.axis_index("zl")).astype(jnp.int32)
    me = tensor_index.reshape(1)
    place = jnp.stack([lax.axis_index("zh"), lax.axis_index("x"), lax.axis_index("c")]).astype(
        jnp.int32
    )
    patch_rows, width = patches.shape
    rows = patch_rows * TENSOR
    own = image_permute(patches)

    dec_rows = dec_hidden.shape[0]
    depth, steps = 1024, 4
    dec_width, query_width = query_weight.shape
    fixed = lambda shape: pl.BlockSpec(shape, lambda i: (0, 0))
    gain_view = dec_gain.reshape(1, -1)
    begun, inverse = pl.pallas_call(
        query_first_kernel,
        grid=(steps,),
        out_shape=(
            jax.ShapeDtypeStruct((dec_rows, query_width), F32),
            jax.ShapeDtypeStruct((dec_rows, 128), F32),
        ),
        in_specs=[
            fixed((dec_rows, dec_width)),
            fixed((1, dec_width)),
            pl.BlockSpec((depth, query_width), lambda i: (i, 0)),
        ],
        out_specs=(fixed((dec_rows, query_width)), fixed((dec_rows, 128))),
        compiler_params=limits(56),
    )(dec_hidden, gain_view, query_weight)
    message = pl.pallas_call(
        query_last_kernel,
        grid=(steps,),
        out_shape=jax.ShapeDtypeStruct((dec_rows + 16, query_width), BF16),
        in_specs=[
            pl.BlockSpec((dec_rows, dec_width // 2), lambda i: (0, 1)),
            pl.BlockSpec((1, dec_width // 2), lambda i: (0, 1)),
            pl.BlockSpec((depth, query_width), lambda i: (i + steps, 0)),
            fixed((dec_rows, query_width)),
            fixed((dec_rows, 128)),
            fixed((1, HD)),
            fixed((1, dec_rows)),
            fixed((1, dec_rows)),
        ],
        out_specs=fixed((dec_rows + 16, query_width)),
        scratch_shapes=[pltpu.VMEM((dec_rows, query_width), F32)],
        compiler_params=limits(56),
    )(
        dec_hidden,
        gain_view,
        query_weight,
        begun,
        inverse,
        query_gain.reshape(1, -1),
        image_of_row.reshape(1, -1),
        valid_count.reshape(1, -1),
    )

    owner = lax.axis_index("c") * XS + lax.axis_index("x")
    share = lax.dynamic_slice_in_dim(enc_out, owner * SHARE, SHARE, axis=0)
    share = jnp.pad(share, ((0, 24 - SHARE), (0, 0)))
    gain_row = enc_gain.reshape(1, -1)
    pieces = gather_tensor(jnp.concatenate([own, share], axis=0))
    q, kv, base = pl.pallas_call(
        qkv_kernel,
        out_shape=(
            jax.ShapeDtypeStruct((2, rows, EHD), BF16),
            jax.ShapeDtypeStruct((4 * EHD + TENSOR * SHARE, rows), BF16),
            jax.ShapeDtypeStruct((rows, 2 * HD), F32),
        ),
        in_specs=[smem()] + vmem(TENSOR + 3),
        out_specs=tuple(vmem(3)),
        scratch_shapes=[
            pltpu.VMEM((rows, width), BF16),
            pltpu.VMEM((rows, width), BF16),
            pltpu.VMEM((TENSOR * SLOT, width), BF16),
        ],
        compiler_params=limits(16),
    )(me, *pieces, gain_row, enc_qkv.transpose(0, 2, 1), cross_kv)
    kv_pieces = gather_xc(kv)
    every_query = [message] + [xor_permute(message, "zh", ZH, k) for k in range(1, ZH)]

    attended = pl.pallas_call(
        encoder_kernel,
        out_shape=jax.ShapeDtypeStruct((2 * EHD, rows), BF16),
        in_specs=vmem(9),
        out_specs=vmem(1)[0],
        scratch_shapes=[pltpu.VMEM((2, rows, 8 * rows), F32)],
        compiler_params=limits(20),
    )(q, *kv_pieces)
    attended_pieces = gather_tensor(attended)
    folded = pl.pallas_call(
        fold_kernel,
        out_shape=jax.ShapeDtypeStruct((TENSOR, 2 * EHD, 2 * HD), BF16),
        in_specs=[smem()] + vmem(8),
        out_specs=vmem(1)[0],
        scratch_shapes=[pltpu.VMEM((TENSOR * 2 * EHD, 2 * HD), BF16)],
        compiler_params=limits(16),
    )(place, *kv_pieces)
    slab = pl.pallas_call(
        cross_kernel,
        out_shape=jax.ShapeDtypeStruct((rows, 2 * HD), BF16),
        in_specs=[smem()] + vmem(TENSOR + 3),
        out_specs=vmem(1)[0],
        compiler_params=limits(12),
    )(me, *attended_pieces, folded, base, key_gain.reshape(1, -1))
    slabs = gather_xc(slab)
    result = None
    for k in (2, 1, 3, 0):
        out = pl.pallas_call(
            decode_kernel,
            out_shape=jax.ShapeDtypeStruct((dec_rows, 4 * HD), BF16),
            in_specs=[smem()] + vmem(9),
            out_specs=vmem(1)[0],
            compiler_params=limits(12),
        )(place, every_query[k], *slabs)
        if k:
            out = xor_permute(out, "zh", ZH, k)
        result = out if result is None else result + out
    return result


def solution(mesh):
    parts = Mesh(mesh.devices.reshape(ZH, CORES, YS, ZL, XS), ("zh", "c", "y", "zl", "x"))
    group, tensor, seq = ("zh", "c"), ("y", "zl"), ("x",)
    in_specs = (
        P(group + tensor + seq, None),
        P(),
        P(None, None, tensor),
        P(tensor, None),
        P(None, tensor),
        P(),
        P(group + seq, None),
        P(),
        P(None, tensor),
        P(),
        P(group + seq),
        P(group + seq),
    )
    out_specs = P(group + seq, tensor)

    return jax.shard_map(
        on_device, mesh=parts, in_specs=in_specs, out_specs=out_specs, check_vma=False
    )
```

```python
import math

import jax
import jax.numpy as jnp
from jax import lax
from jax.experimental import pallas as pl
from jax.experimental.pallas import tpu as pltpu
from jax.sharding import Mesh
from jax.sharding import PartitionSpec as P

EHD = 80
HD = 128
EPSILON = 1e-05
F32 = jnp.float32
BF16 = jnp.bfloat16
ZH, CORES, YS, ZL, XS = 4, 2, 4, 2, 4
SHARE, SLOT = 20, 32
TENSOR_ORDER, X_ORDER = (5, 7, 3, 4, 6, 2, 1), (2, 3, 1)
TENSOR = YS * ZL
NT = (((1,), (1,)), ((), ()))


def vmem(count):
    return [pl.BlockSpec(memory_space=pltpu.VMEM)] * count


def smem():
    return pl.BlockSpec(memory_space=pltpu.SMEM)


def xor_permute(values, axes, size, step):
    return lax.ppermute(values, axes, [(i, i ^ step) for i in range(size)])


def image_permute(values):
    pairs = []
    for zh in range(ZH):
        for y in range(YS):
            for zl in range(ZL):
                image, slot = (y % 2) * 2 + zl, (y // 2) * ZH + zh
                pairs.append(((zh * YS + y) * ZL + zl, image * TENSOR + slot))
    return lax.ppermute(values, ("zh", "y", "zl"), pairs)


def qkv_kernel(me_ref, *refs):
    pieces, refs = refs[:TENSOR], refs[TENSOR:]
    gain_ref, weight_ref, cross_ref, q_ref, kv_ref, base_ref, normed, raw, out_rows = refs
    me = me_ref[0]
    rows = raw.shape[0] // TENSOR
    for step in range(TENSOR):
        piece = pieces[step][:rows, :]
        values = piece.astype(F32)
        mean_value = jnp.mean(values, axis=-1, keepdims=True)
        centered = values - mean_value
        variance = jnp.mean(centered * centered, axis=-1, keepdims=True)
        result = centered * lax.rsqrt(variance + EPSILON) * gain_ref[...]
        place = pl.ds(pl.multiple_of(jnp.bitwise_xor(me, step) * rows, rows), rows)
        normed[place, :] = result.astype(BF16)
        raw[place, :] = piece
        share = pieces[step][rows:, :]
        fill = jnp.zeros((SLOT - share.shape[0], share.shape[1]), BF16)
        place = pl.ds(pl.multiple_of(jnp.bitwise_xor(me, step) * SLOT, SLOT), SLOT)
        out_rows[place, :] = jnp.concatenate([share, fill], axis=0)
    x = normed[...]
    width = 2 * EHD
    for part in range(2):
        out = lax.dot_general(weight_ref[1 + part], x, NT, preferred_element_type=F32)
        kv_ref[part * width : (part + 1) * width, :] = out.astype(BF16)
    q = lax.dot_general(x, weight_ref[0], NT, preferred_element_type=F32)
    for head in range(2):
        q_ref[head] = q[:, head * EHD : (head + 1) * EHD].astype(BF16)
    cross = cross_ref[...]
    fold = jnp.dot(out_rows[...], cross, preferred_element_type=F32)
    row = lax.broadcasted_iota(jnp.int32, (TENSOR * SHARE, TENSOR * SLOT), 0)
    column = lax.broadcasted_iota(jnp.int32, (TENSOR * SHARE, TENSOR * SLOT), 1)
    chosen = (column == row + ((row * 3277) >> 16) * (SLOT - SHARE)).astype(F32).astype(BF16)
    fold = jnp.dot(chosen, fold.astype(BF16), preferred_element_type=F32)
    kv_ref[4 * EHD :, :] = fold.astype(BF16)
    base_ref[...] = jnp.dot(raw[...], cross, preferred_element_type=F32)


def encoder_kernel(q_ref, *refs):
    count = 8
    pieces, (out_ref, scores) = refs[:count], refs[count:]
    rows = q_ref.shape[1]
    scale = 1.0 / math.sqrt(EHD)
    for head in range(2):
        q = q_ref[head]
        top = None
        for j in range(count):
            s = jnp.dot(q, pieces[j][head * EHD : (head + 1) * EHD, :], preferred_element_type=F32)
            scores[head, :, j * rows : (j + 1) * rows] = s
            part = jnp.maximum(s[:, :128], s[:, 128:])
            top = part if top is None else jnp.maximum(top, part)
        top = jnp.max(top, axis=-1, keepdims=True)
        mix = jnp.zeros((rows, EHD), F32)
        total = jnp.zeros((rows, 128), F32)
        low = 2 * EHD + head * EHD
        for j in range(count):
            p = jnp.exp((scores[head, :, j * rows : (j + 1) * rows] - top) * scale)
            total = total + (p[:, :128] + p[:, 128:])
            mix = mix + lax.dot_general(
                p.astype(BF16), pieces[j][low : low + EHD, :], NT, preferred_element_type=F32
            )
        attended = mix / jnp.sum(total, axis=-1, keepdims=True)
        out_ref[head * EHD : (head + 1) * EHD, :] = attended.T.astype(BF16)


def fold_kernel(place_ref, *refs):
    pieces, (out_ref, stacked) = refs[:8], refs[8:]
    x, c = place_ref[1], place_ref[2]
    size = TENSOR * SHARE
    for k in range(8):
        owner = jnp.bitwise_xor(c, k // 4) * 4 + jnp.bitwise_xor(x, k % 4)
        low = pl.multiple_of(owner * size, size)
        stacked[pl.ds(low, size), :] = pieces[k][4 * EHD :, :]
    for t in range(TENSOR):
        row = lax.broadcasted_iota(jnp.int32, (size, 8 * size), 0)
        column = lax.broadcasted_iota(jnp.int32, (size, 8 * size), 1)
        owner = (row * 3277) >> 16
        source = owner * (size - SHARE) + row + t * SHARE
        chosen = (column == source).astype(F32).astype(BF16)
        out = jnp.dot(chosen, stacked[...], preferred_element_type=F32)
        out_ref[t] = out.astype(BF16)


def cross_kernel(me_ref, *refs):
    pieces, (weight_ref, base_ref, gain_ref, out_ref) = refs[:TENSOR], refs[TENSOR:]
    me = me_ref[0]
    proj = base_ref[...]
    for step in range(TENSOR):
        weight = weight_ref[jnp.bitwise_xor(me, step)]
        proj = proj + lax.dot_general(
            pieces[step][...], weight, (((0,), (0,)), ((), ())), preferred_element_type=F32
        )
    keys = proj[:, :HD]
    square_mean = jnp.mean(keys * keys, axis=-1, keepdims=True)
    keys = keys * lax.rsqrt(square_mean + EPSILON) * gain_ref[...]
    out_ref[:, :HD] = keys.astype(BF16)
    out_ref[:, HD:] = proj[:, HD:].astype(BF16)


def query_part(x_ref, gain_ref, weight_ref, total, inverse, step):
    depth = weight_ref.shape[0]
    columns = pl.ds(pl.multiple_of(step * depth, depth), depth)
    normed = x_ref[:, columns].astype(F32) * inverse[:, 0:1] * gain_ref[:, columns]
    total[...] += jnp.dot(normed.astype(BF16), weight_ref[...], preferred_element_type=F32)


def query_first_kernel(x_ref, gain_ref, weight_ref, total, inverse):
    @pl.when(pl.program_id(0) == 0)
    def _():
        square = jnp.zeros((x_ref.shape[0], 128), F32)
        for low in range(0, x_ref.shape[1], 128):
            part = x_ref[:, low : low + 128].astype(F32)
            square = square + part * part
        mean = jnp.sum(square, axis=-1, keepdims=True) / x_ref.shape[1]
        inverse[...] = jnp.broadcast_to(lax.rsqrt(mean + EPSILON), inverse.shape)
        total[...] = jnp.zeros_like(total)

    query_part(x_ref, gain_ref, weight_ref, total, inverse, pl.program_id(0))


def query_last_kernel(
    x_ref, gain_ref, weight_ref, begun, inverse, head_gain_ref, image_ref, count_ref, out_ref, total
):
    rows = x_ref.shape[0]

    @pl.when(pl.program_id(0) == 0)
    def _():
        total[...] = begun[...]

    query_part(x_ref, gain_ref, weight_ref, total, inverse, 0)

    @pl.when(pl.program_id(0) == pl.num_programs(0) - 1)
    def _():
        for head in range(4):
            q = total[:, head * HD : (head + 1) * HD]
            mean = jnp.mean(q * q, axis=-1, keepdims=True)
            q = q * lax.rsqrt(mean + EPSILON) * head_gain_ref[...] / math.sqrt(HD)
            out_ref[:rows, head * HD : (head + 1) * HD] = q.astype(BF16)
        count = count_ref[...]
        extra = jnp.concatenate([image_ref[...], count >> 4, count & 15], axis=0)
        extra = jnp.concatenate([extra, jnp.zeros((13, rows), jnp.int32)], axis=0)
        out_ref[rows:, :rows] = extra.astype(F32).astype(BF16)
        out_ref[rows:, rows:] = jnp.zeros((16, out_ref.shape[1] - rows), BF16)


def decode_kernel(place_ref, query_ref, *refs):
    slabs, out_ref = refs[:8], refs[8]
    keys = slabs[0].shape[0]
    zh, x, c = place_ref[0], place_ref[1], place_ref[2]
    lane = lax.broadcasted_iota(jnp.int32, (1, keys), 1)
    base = ((lane >> 5) & 3) * 512 + (lane >> 7) * 128 + (lane & 31)
    rows = out_ref.shape[0]
    extra = query_ref[rows : rows + 8, :HD].astype(F32)
    limit = jnp.where(extra[0:1] == zh.astype(F32), extra[1:2] * 16.0 + extra[2:3], 0.0)
    limit = jnp.broadcast_to(limit, (8, rows)).T[:, 0:1]
    limit = jnp.concatenate([limit] * 4, axis=0)
    q = [query_ref[:rows, head * HD : (head + 1) * HD] for head in range(4)]
    q = jnp.concatenate(q, axis=0)
    mix = jnp.zeros((4 * rows, HD), F32)
    total = jnp.zeros((4 * rows, 128), F32)
    for j in range(8):
        px = jnp.bitwise_xor(x, j % 4)
        pc = jnp.bitwise_xor(c, j // 4)
        pos = (base + (pc * 256 + px * 32)).astype(F32)
        s = lax.dot_general(q, slabs[j][:, :HD], NT, preferred_element_type=F32)
        w = jnp.where(pos < limit, jnp.exp(s), 0.0)
        total = total + (w[:, :128] + w[:, 128:])
        mix = mix + jnp.dot(w.astype(BF16), slabs[j][:, HD:], preferred_element_type=F32)
    total = jnp.sum(total, axis=-1, keepdims=True)
    mix = mix / jnp.where(total > 0.0, total, 1.0)
    for head in range(4):
        part = mix[head * rows : (head + 1) * rows]
        out_ref[:, head * HD : (head + 1) * HD] = part.astype(BF16)


def limits(mib):
    return pltpu.CompilerParams(vmem_limit_bytes=mib << 20)


def gather_xc(piece):
    along_x = {0: piece}
    for k in X_ORDER:
        along_x[k] = xor_permute(piece, "x", XS, k)
    along_x = [along_x[k] for k in range(XS)]
    return along_x + [xor_permute(value, "c", CORES, 1) for value in along_x]


def gather_tensor(piece):
    pieces = {0: piece}
    for k in TENSOR_ORDER:
        pieces[k] = xor_permute(piece, ("y", "zl"), TENSOR, k)
    return [pieces[k] for k in range(TENSOR)]


def on_device(
    patches,
    enc_gain,
    enc_qkv,
    enc_out,
    cross_kv,
    key_gain,
    dec_hidden,
    dec_gain,
    query_weight,
    query_gain,
    image_of_row,
    valid_count,
):
    tensor_index = (lax.axis_index("y") * ZL + lax.axis_index("zl")).astype(jnp.int32)
    me = tensor_index.reshape(1)
    place = jnp.stack([lax.axis_index("zh"), lax.axis_index("x"), lax.axis_index("c")]).astype(
        jnp.int32
    )
    patch_rows, width = patches.shape
    rows = patch_rows * TENSOR
    own = image_permute(patches)

    dec_rows = dec_hidden.shape[0]
    depth, first_steps, last_steps = 1024, 2, 6
    dec_width, query_width = query_weight.shape
    fixed = lambda shape: pl.BlockSpec(shape, lambda i: (0, 0))
    gain_view = dec_gain.reshape(1, -1)
    begun, inverse = pl.pallas_call(
        query_first_kernel,
        grid=(first_steps,),
        out_shape=(
            jax.ShapeDtypeStruct((dec_rows, query_width), F32),
            jax.ShapeDtypeStruct((dec_rows, 128), F32),
        ),
        in_specs=[
            fixed((dec_rows, dec_width)),
            fixed((1, dec_width)),
            pl.BlockSpec((depth, query_width), lambda i: (i, 0)),
        ],
        out_specs=(fixed((dec_rows, query_width)), fixed((dec_rows, 128))),
        compiler_params=limits(56),
    )(dec_hidden, gain_view, query_weight)
    message = pl.pallas_call(
        query_last_kernel,
        grid=(last_steps,),
        out_shape=jax.ShapeDtypeStruct((dec_rows + 16, query_width), BF16),
        in_specs=[
            pl.BlockSpec((dec_rows, depth), lambda i: (0, i + first_steps)),
            pl.BlockSpec((1, depth), lambda i: (0, i + first_steps)),
            pl.BlockSpec((depth, query_width), lambda i: (i + first_steps, 0)),
            fixed((dec_rows, query_width)),
            fixed((dec_rows, 128)),
            fixed((1, HD)),
            fixed((1, dec_rows)),
            fixed((1, dec_rows)),
        ],
        out_specs=fixed((dec_rows + 16, query_width)),
        scratch_shapes=[pltpu.VMEM((dec_rows, query_width), F32)],
        compiler_params=limits(56),
    )(
        dec_hidden,
        gain_view,
        query_weight,
        begun,
        inverse,
        query_gain.reshape(1, -1),
        image_of_row.reshape(1, -1),
        valid_count.reshape(1, -1),
    )

    owner = lax.axis_index("c") * XS + lax.axis_index("x")
    share = lax.dynamic_slice_in_dim(enc_out, owner * SHARE, SHARE, axis=0)
    share = jnp.pad(share, ((0, 24 - SHARE), (0, 0)))
    gain_row = enc_gain.reshape(1, -1)
    pieces = gather_tensor(jnp.concatenate([own, share], axis=0))
    q, kv, base = pl.pallas_call(
        qkv_kernel,
        out_shape=(
            jax.ShapeDtypeStruct((2, rows, EHD), BF16),
            jax.ShapeDtypeStruct((4 * EHD + TENSOR * SHARE, rows), BF16),
            jax.ShapeDtypeStruct((rows, 2 * HD), F32),
        ),
        in_specs=[smem()] + vmem(TENSOR + 3),
        out_specs=tuple(vmem(3)),
        scratch_shapes=[
            pltpu.VMEM((rows, width), BF16),
            pltpu.VMEM((rows, width), BF16),
            pltpu.VMEM((TENSOR * SLOT, width), BF16),
        ],
        compiler_params=limits(16),
    )(me, *pieces, gain_row, enc_qkv.transpose(0, 2, 1), cross_kv)
    kv_pieces = gather_xc(kv)
    every_query = [message] + [xor_permute(message, "zh", ZH, k) for k in range(1, ZH)]

    attended = pl.pallas_call(
        encoder_kernel,
        out_shape=jax.ShapeDtypeStruct((2 * EHD, rows), BF16),
        in_specs=vmem(9),
        out_specs=vmem(1)[0],
        scratch_shapes=[pltpu.VMEM((2, rows, 8 * rows), F32)],
        compiler_params=limits(20),
    )(q, *kv_pieces)
    attended_pieces = gather_tensor(attended)
    folded = pl.pallas_call(
        fold_kernel,
        out_shape=jax.ShapeDtypeStruct((TENSOR, 2 * EHD, 2 * HD), BF16),
        in_specs=[smem()] + vmem(8),
        out_specs=vmem(1)[0],
        scratch_shapes=[pltpu.VMEM((TENSOR * 2 * EHD, 2 * HD), BF16)],
        compiler_params=limits(16),
    )(place, *kv_pieces)
    slab = pl.pallas_call(
        cross_kernel,
        out_shape=jax.ShapeDtypeStruct((rows, 2 * HD), BF16),
        in_specs=[smem()] + vmem(TENSOR + 3),
        out_specs=vmem(1)[0],
        compiler_params=limits(12),
    )(me, *attended_pieces, folded, base, key_gain.reshape(1, -1))
    slabs = gather_xc(slab)
    result = None
    for k in (2, 1, 3, 0):
        out = pl.pallas_call(
            decode_kernel,
            out_shape=jax.ShapeDtypeStruct((dec_rows, 4 * HD), BF16),
            in_specs=[smem()] + vmem(9),
            out_specs=vmem(1)[0],
            compiler_params=limits(12),
        )(place, every_query[k], *slabs)
        if k:
            out = xor_permute(out, "zh", ZH, k)
        result = out if result is None else result + out
    return result


def solution(mesh):
    parts = Mesh(mesh.devices.reshape(ZH, CORES, YS, ZL, XS), ("zh", "c", "y", "zl", "x"))
    group, tensor, seq = ("zh", "c"), ("y", "zl"), ("x",)
    in_specs = (
        P(group + tensor + seq, None),
        P(),
        P(None, None, tensor),
        P(tensor, None),
        P(None, tensor),
        P(),
        P(group + seq, None),
        P(),
        P(None, tensor),
        P(),
        P(group + seq),
        P(group + seq),
    )
    out_specs = P(group + seq, tensor)

    return jax.shard_map(
        on_device, mesh=parts, in_specs=in_specs, out_specs=out_specs, check_vma=False
    )
```

```python
import math

import jax
import jax.numpy as jnp
from jax import lax
from jax.experimental import pallas as pl
from jax.experimental.pallas import tpu as pltpu
from jax.sharding import Mesh
from jax.sharding import PartitionSpec as P

EHD = 80
HD = 128
EPSILON = 1e-05
F32 = jnp.float32
BF16 = jnp.bfloat16
ZH, CORES, YS, ZL, XS = 4, 2, 4, 2, 4
SHARE, SLOT, STREAMS = 20, 32, 4
TENSOR_ORDER, X_ORDER = (5, 7, 3, 4, 6, 2, 1), (2, 3, 1)
TENSOR = YS * ZL
NT = (((1,), (1,)), ((), ()))


def vmem(count):
    return [pl.BlockSpec(memory_space=pltpu.VMEM)] * count


def smem():
    return pl.BlockSpec(memory_space=pltpu.SMEM)


def xor_permute(values, axes, size, step):
    return lax.ppermute(values, axes, [(i, i ^ step) for i in range(size)])


def image_permute(values):
    pairs = []
    for zh in range(ZH):
        for y in range(YS):
            for zl in range(ZL):
                image, slot = (y % 2) * 2 + zl, (y // 2) * ZH + zh
                pairs.append(((zh * YS + y) * ZL + zl, image * TENSOR + slot))
    return lax.ppermute(values, ("zh", "y", "zl"), pairs)


def qkv_kernel(me_ref, *refs):
    pieces, refs = refs[:TENSOR], refs[TENSOR:]
    gain_ref, weight_ref, cross_ref, q_ref, kv_ref, base_ref, normed, raw, out_rows = refs
    me = me_ref[0]
    rows = raw.shape[0] // TENSOR
    for step in range(TENSOR):
        piece = pieces[step][:rows, :]
        values = piece.astype(F32)
        mean_value = jnp.mean(values, axis=-1, keepdims=True)
        centered = values - mean_value
        variance = jnp.mean(centered * centered, axis=-1, keepdims=True)
        result = centered * lax.rsqrt(variance + EPSILON) * gain_ref[...]
        place = pl.ds(pl.multiple_of(jnp.bitwise_xor(me, step) * rows, rows), rows)
        normed[place, :] = result.astype(BF16)
        raw[place, :] = piece
        share = pieces[step][rows:, :]
        fill = jnp.zeros((SLOT - share.shape[0], share.shape[1]), BF16)
        place = pl.ds(pl.multiple_of(jnp.bitwise_xor(me, step) * SLOT, SLOT), SLOT)
        out_rows[place, :] = jnp.concatenate([share, fill], axis=0)
    x = normed[...]
    width = 2 * EHD
    for part in range(2):
        out = lax.dot_general(weight_ref[1 + part], x, NT, preferred_element_type=F32)
        kv_ref[part * width : (part + 1) * width, :] = out.astype(BF16)
    q = lax.dot_general(x, weight_ref[0], NT, preferred_element_type=F32)
    for head in range(2):
        q_ref[head] = q[:, head * EHD : (head + 1) * EHD].astype(BF16)
    cross = cross_ref[...]
    fold = jnp.dot(out_rows[...], cross, preferred_element_type=F32)
    row = lax.broadcasted_iota(jnp.int32, (TENSOR * SHARE, TENSOR * SLOT), 0)
    column = lax.broadcasted_iota(jnp.int32, (TENSOR * SHARE, TENSOR * SLOT), 1)
    chosen = (column == row + ((row * 3277) >> 16) * (SLOT - SHARE)).astype(F32).astype(BF16)
    fold = jnp.dot(chosen, fold.astype(BF16), preferred_element_type=F32)
    kv_ref[4 * EHD :, :] = fold.astype(BF16)
    base_ref[...] = jnp.dot(raw[...], cross, preferred_element_type=F32)


def encoder_kernel(q_ref, *refs):
    count = 8
    pieces, (out_ref, scores) = refs[:count], refs[count:]
    rows = q_ref.shape[1]
    scale = 1.0 / math.sqrt(EHD)
    for head in range(2):
        q = q_ref[head]
        top = None
        for j in range(count):
            s = jnp.dot(q, pieces[j][head * EHD : (head + 1) * EHD, :], preferred_element_type=F32)
            scores[head, :, j * rows : (j + 1) * rows] = s
            part = jnp.maximum(s[:, :128], s[:, 128:])
            top = part if top is None else jnp.maximum(top, part)
        top = jnp.max(top, axis=-1, keepdims=True)
        mix = jnp.zeros((rows, EHD), F32)
        total = jnp.zeros((rows, 128), F32)
        low = 2 * EHD + head * EHD
        for j in range(count):
            p = jnp.exp((scores[head, :, j * rows : (j + 1) * rows] - top) * scale)
            total = total + (p[:, :128] + p[:, 128:])
            mix = mix + lax.dot_general(
                p.astype(BF16), pieces[j][low : low + EHD, :], NT, preferred_element_type=F32
            )
        attended = mix / jnp.sum(total, axis=-1, keepdims=True)
        out_ref[head * EHD : (head + 1) * EHD, :] = attended.T.astype(BF16)


def fold_kernel(place_ref, *refs):
    pieces, (out_ref, stacked) = refs[:8], refs[8:]
    x, c = place_ref[1], place_ref[2]
    size = TENSOR * SHARE
    for k in range(8):
        owner = jnp.bitwise_xor(c, k // 4) * 4 + jnp.bitwise_xor(x, k % 4)
        low = pl.multiple_of(owner * size, size)
        stacked[pl.ds(low, size), :] = pieces[k][4 * EHD :, :]
    for t in range(TENSOR):
        row = lax.broadcasted_iota(jnp.int32, (size, 8 * size), 0)
        column = lax.broadcasted_iota(jnp.int32, (size, 8 * size), 1)
        owner = (row * 3277) >> 16
        source = owner * (size - SHARE) + row + t * SHARE
        chosen = (column == source).astype(F32).astype(BF16)
        out = jnp.dot(chosen, stacked[...], preferred_element_type=F32)
        out_ref[t] = out.astype(BF16)


def cross_kernel(me_ref, *refs):
    pieces, (weight_ref, base_ref, gain_ref, out_ref) = refs[:TENSOR], refs[TENSOR:]
    me = me_ref[0]
    proj = base_ref[...]
    for step in range(TENSOR):
        weight = weight_ref[jnp.bitwise_xor(me, step)]
        proj = proj + lax.dot_general(
            pieces[step][...], weight, (((0,), (0,)), ((), ())), preferred_element_type=F32
        )
    keys = proj[:, :HD]
    square_mean = jnp.mean(keys * keys, axis=-1, keepdims=True)
    keys = keys * lax.rsqrt(square_mean + EPSILON) * gain_ref[...]
    out_ref[:, :HD] = keys.astype(BF16)
    out_ref[:, HD:] = proj[:, HD:].astype(BF16)


def query_part(x_ref, gain_ref, weights, total, inverse, step):
    depth = weights[0].shape[0]
    out = total[...]
    for k, weight_ref in enumerate(weights):
        low = (step * STREAMS + k) * depth
        columns = pl.ds(pl.multiple_of(low, depth), depth)
        normed = x_ref[:, columns].astype(F32) * inverse[:, 0:1] * gain_ref[:, columns]
        out = out + jnp.dot(normed.astype(BF16), weight_ref[...], preferred_element_type=F32)
    total[...] = out


def query_first_kernel(x_ref, gain_ref, *refs):
    weights, (total, inverse) = refs[:STREAMS], refs[STREAMS:]

    @pl.when(pl.program_id(0) == 0)
    def _():
        square = jnp.zeros((x_ref.shape[0], 128), F32)
        for low in range(0, x_ref.shape[1], 128):
            part = x_ref[:, low : low + 128].astype(F32)
            square = square + part * part
        mean = jnp.sum(square, axis=-1, keepdims=True) / x_ref.shape[1]
        inverse[...] = jnp.broadcast_to(lax.rsqrt(mean + EPSILON), inverse.shape)
        total[...] = jnp.zeros_like(total)

    query_part(x_ref, gain_ref, weights, total, inverse, pl.program_id(0))


def query_last_kernel(x_ref, gain_ref, *refs):
    weights, refs = refs[:STREAMS], refs[STREAMS:]
    begun, inverse, head_gain_ref, image_ref, count_ref, out_ref, total = refs
    rows = x_ref.shape[0]

    @pl.when(pl.program_id(0) == 0)
    def _():
        total[...] = begun[...]

    query_part(x_ref, gain_ref, weights, total, inverse, 0)

    @pl.when(pl.program_id(0) == pl.num_programs(0) - 1)
    def _():
        for head in range(4):
            q = total[:, head * HD : (head + 1) * HD]
            mean = jnp.mean(q * q, axis=-1, keepdims=True)
            q = q * lax.rsqrt(mean + EPSILON) * head_gain_ref[...] / math.sqrt(HD)
            out_ref[:rows, head * HD : (head + 1) * HD] = q.astype(BF16)
        count = count_ref[...]
        extra = jnp.concatenate([image_ref[...], count >> 4, count & 15], axis=0)
        extra = jnp.concatenate([extra, jnp.zeros((13, rows), jnp.int32)], axis=0)
        out_ref[rows:, :rows] = extra.astype(F32).astype(BF16)
        out_ref[rows:, rows:] = jnp.zeros((16, out_ref.shape[1] - rows), BF16)


def decode_rows(q, limit, first, slabs):
    keys = slabs[0].shape[0]
    lane = lax.broadcasted_iota(jnp.int32, (1, keys), 1)
    base = ((lane >> 5) & 3) * 512 + (lane >> 7) * 128 + (lane & 31)
    mix = jnp.zeros((q.shape[0], HD), F32)
    total = jnp.zeros((q.shape[0], 128), F32)
    for j in range(8):
        pos = (base + first[j]).astype(F32)
        s = lax.dot_general(q, slabs[j][:, :HD], NT, preferred_element_type=F32)
        w = jnp.where(pos < limit, jnp.exp(s), 0.0)
        total = total + (w[:, :128] + w[:, 128:])
        mix = mix + jnp.dot(w.astype(BF16), slabs[j][:, HD:], preferred_element_type=F32)
    total = jnp.sum(total, axis=-1, keepdims=True)
    return (mix / jnp.where(total > 0.0, total, 1.0)).astype(BF16)


def decode_kernel(place_ref, query_ref, *refs):
    slabs, out_ref = refs[:8], refs[8]
    rows = out_ref.shape[0]
    few = rows // 2
    zh, x, c = place_ref[0], place_ref[1], place_ref[2]
    first = [jnp.bitwise_xor(c, j // 4) * 256 + jnp.bitwise_xor(x, j % 4) * 32 for j in range(8)]
    extra = query_ref[rows : rows + 8, :HD].astype(F32)
    mine = extra[0:1] == zh.astype(F32)
    limit = jnp.where(mine, extra[1:2] * 16.0 + extra[2:3], 0.0)
    member = mine.astype(F32)
    count = jnp.sum(member)

    @pl.when(count <= few)
    def _():
        below = lax.broadcasted_iota(jnp.int32, (rows, rows), 0)
        below = below < lax.broadcasted_iota(jnp.int32, (rows, rows), 1)
        rank = jnp.dot(
            jnp.broadcast_to(member, (8, rows)).astype(BF16),
            below.astype(F32).astype(BF16),
            preferred_element_type=F32,
        )[0:1]
        slot = lax.broadcasted_iota(jnp.int32, (few, rows), 0).astype(F32)
        chosen = jnp.where(rank == slot, member, 0.0)
        picked = chosen.astype(BF16)
        q = jnp.dot(picked, query_ref[:rows, :], preferred_element_type=F32).astype(BF16)
        q = jnp.concatenate([q[:, head * HD : (head + 1) * HD] for head in range(4)], axis=0)
        bound = jnp.sum(chosen * limit, axis=-1, keepdims=True)
        out = decode_rows(q, jnp.concatenate([bound] * 4, axis=0), first, slabs)
        out = jnp.concatenate([out[head * few : (head + 1) * few] for head in range(4)], axis=1)
        back = chosen.T.astype(BF16)
        out_ref[...] = jnp.dot(back, out, preferred_element_type=F32).astype(BF16)

    @pl.when(count > few)
    def _():
        bound = jnp.broadcast_to(limit, (8, rows)).T[:, 0:1]
        q = [query_ref[:rows, head * HD : (head + 1) * HD] for head in range(4)]
        q = jnp.concatenate(q, axis=0)
        out = decode_rows(q, jnp.concatenate([bound] * 4, axis=0), first, slabs)
        for head in range(4):
            out_ref[:, head * HD : (head + 1) * HD] = out[head * rows : (head + 1) * rows]


def limits(mib):
    return pltpu.CompilerParams(vmem_limit_bytes=mib << 20)


def gather_xc(piece):
    along_x = {0: piece}
    for k in X_ORDER:
        along_x[k] = xor_permute(piece, "x", XS, k)
    along_x = [along_x[k] for k in range(XS)]
    return along_x + [xor_permute(value, "c", CORES, 1) for value in along_x]


def gather_tensor(piece):
    pieces = {0: piece}
    for k in TENSOR_ORDER:
        pieces[k] = xor_permute(piece, ("y", "zl"), TENSOR, k)
    return [pieces[k] for k in range(TENSOR)]


def on_device(
    patches,
    enc_gain,
    enc_qkv,
    enc_out,
    cross_kv,
    key_gain,
    dec_hidden,
    dec_gain,
    query_weight,
    query_gain,
    image_of_row,
    valid_count,
):
    tensor_index = (lax.axis_index("y") * ZL + lax.axis_index("zl")).astype(jnp.int32)
    me = tensor_index.reshape(1)
    place = jnp.stack([lax.axis_index("zh"), lax.axis_index("x"), lax.axis_index("c")]).astype(
        jnp.int32
    )
    patch_rows, width = patches.shape
    rows = patch_rows * TENSOR
    own = image_permute(patches)

    dec_rows = dec_hidden.shape[0]
    depth, first_steps, last_steps = 1024, 2, 6
    dec_width, query_width = query_weight.shape
    fixed = lambda shape: pl.BlockSpec(shape, lambda i: (0, 0))
    gain_view = dec_gain.reshape(1, -1)
    weights = [query_weight] * STREAMS

    def weight_blocks(begin):
        shape = (depth // STREAMS, query_width)
        return [
            pl.BlockSpec(shape, lambda i, k=k: ((i + begin) * STREAMS + k, 0))
            for k in range(STREAMS)
        ]

    begun, inverse = pl.pallas_call(
        query_first_kernel,
        grid=(first_steps,),
        out_shape=(
            jax.ShapeDtypeStruct((dec_rows, query_width), F32),
            jax.ShapeDtypeStruct((dec_rows, 128), F32),
        ),
        in_specs=[
            fixed((dec_rows, dec_width)),
            fixed((1, dec_width)),
        ]
        + weight_blocks(0),
        out_specs=(fixed((dec_rows, query_width)), fixed((dec_rows, 128))),
        compiler_params=limits(56),
    )(dec_hidden, gain_view, *weights)
    message = pl.pallas_call(
        query_last_kernel,
        grid=(last_steps,),
        out_shape=jax.ShapeDtypeStruct((dec_rows + 16, query_width), BF16),
        in_specs=[
            pl.BlockSpec((dec_rows, depth), lambda i: (0, i + first_steps)),
            pl.BlockSpec((1, depth), lambda i: (0, i + first_steps)),
            *weight_blocks(first_steps),
            fixed((dec_rows, query_width)),
            fixed((dec_rows, 128)),
            fixed((1, HD)),
            fixed((1, dec_rows)),
            fixed((1, dec_rows)),
        ],
        out_specs=fixed((dec_rows + 16, query_width)),
        scratch_shapes=[pltpu.VMEM((dec_rows, query_width), F32)],
        compiler_params=limits(56),
    )(
        dec_hidden,
        gain_view,
        *weights,
        begun,
        inverse,
        query_gain.reshape(1, -1),
        image_of_row.reshape(1, -1),
        valid_count.reshape(1, -1),
    )

    owner = lax.axis_index("c") * XS + lax.axis_index("x")
    share = lax.dynamic_slice_in_dim(enc_out, owner * SHARE, SHARE, axis=0)
    share = jnp.pad(share, ((0, 24 - SHARE), (0, 0)))
    gain_row = enc_gain.reshape(1, -1)
    pieces = gather_tensor(jnp.concatenate([own, share], axis=0))
    q, kv, base = pl.pallas_call(
        qkv_kernel,
        out_shape=(
            jax.ShapeDtypeStruct((2, rows, EHD), BF16),
            jax.ShapeDtypeStruct((4 * EHD + TENSOR * SHARE, rows), BF16),
            jax.ShapeDtypeStruct((rows, 2 * HD), F32),
        ),
        in_specs=[smem()] + vmem(TENSOR + 3),
        out_specs=tuple(vmem(3)),
        scratch_shapes=[
            pltpu.VMEM((rows, width), BF16),
            pltpu.VMEM((rows, width), BF16),
            pltpu.VMEM((TENSOR * SLOT, width), BF16),
        ],
        compiler_params=limits(16),
    )(me, *pieces, gain_row, enc_qkv.transpose(0, 2, 1), cross_kv)
    kv_pieces = gather_xc(kv)
    every_query = [message] + [xor_permute(message, "zh", ZH, k) for k in range(1, ZH)]

    attended = pl.pallas_call(
        encoder_kernel,
        out_shape=jax.ShapeDtypeStruct((2 * EHD, rows), BF16),
        in_specs=vmem(9),
        out_specs=vmem(1)[0],
        scratch_shapes=[pltpu.VMEM((2, rows, 8 * rows), F32)],
        compiler_params=limits(20),
    )(q, *kv_pieces)
    attended_pieces = gather_tensor(attended)
    folded = pl.pallas_call(
        fold_kernel,
        out_shape=jax.ShapeDtypeStruct((TENSOR, 2 * EHD, 2 * HD), BF16),
        in_specs=[smem()] + vmem(8),
        out_specs=vmem(1)[0],
        scratch_shapes=[pltpu.VMEM((TENSOR * 2 * EHD, 2 * HD), BF16)],
        compiler_params=limits(16),
    )(place, *kv_pieces)
    slab = pl.pallas_call(
        cross_kernel,
        out_shape=jax.ShapeDtypeStruct((rows, 2 * HD), BF16),
        in_specs=[smem()] + vmem(TENSOR + 3),
        out_specs=vmem(1)[0],
        compiler_params=limits(12),
    )(me, *attended_pieces, folded, base, key_gain.reshape(1, -1))
    slabs = gather_xc(slab)
    result = None
    for k in (2, 1, 3, 0):
        out = pl.pallas_call(
            decode_kernel,
            out_shape=jax.ShapeDtypeStruct((dec_rows, 4 * HD), BF16),
            in_specs=[smem()] + vmem(9),
            out_specs=vmem(1)[0],
            compiler_params=limits(12),
        )(place, every_query[k], *slabs)
        if k:
            out = xor_permute(out, "zh", ZH, k)
        result = out if result is None else result + out
    return result


def solution(mesh):
    parts = Mesh(mesh.devices.reshape(ZH, CORES, YS, ZL, XS), ("zh", "c", "y", "zl", "x"))
    group, tensor, seq = ("zh", "c"), ("y", "zl"), ("x",)
    in_specs = (
        P(group + tensor + seq, None),
        P(),
        P(None, None, tensor),
        P(tensor, None),
        P(None, tensor),
        P(),
        P(group + seq, None),
        P(),
        P(None, tensor),
        P(),
        P(group + seq),
        P(group + seq),
    )
    out_specs = P(group + seq, tensor)

    return jax.shard_map(
        on_device, mesh=parts, in_specs=in_specs, out_specs=out_specs, check_vma=False
    )
```

```python
import functools
import math

import jax
import jax.numpy as jnp
from jax import lax
from jax.experimental import pallas as pl
from jax.experimental.pallas import tpu as pltpu
from jax.sharding import Mesh
from jax.sharding import PartitionSpec as P

EHD = 80
HD = 128
EPSILON = 1e-05
F32 = jnp.float32
BF16 = jnp.bfloat16
ZH, CORES, YS, ZL, XS = 4, 2, 4, 2, 4
SHARE, SLOT, STREAMS = 20, 32, 4
TENSOR_ORDER, X_ORDER = (5, 7, 3, 4, 6, 2, 1), (2, 3, 1)
TENSOR = YS * ZL
NT = (((1,), (1,)), ((), ()))


def vmem(count):
    return [pl.BlockSpec(memory_space=pltpu.VMEM)] * count


def smem():
    return pl.BlockSpec(memory_space=pltpu.SMEM)


def xor_permute(values, axes, size, step):
    return lax.ppermute(values, axes, [(i, i ^ step) for i in range(size)])


def image_permute(values):
    pairs = []
    for zh in range(ZH):
        for y in range(YS):
            for zl in range(ZL):
                image, slot = (y % 2) * 2 + zl, (y // 2) * ZH + zh
                pairs.append(((zh * YS + y) * ZL + zl, image * TENSOR + slot))
    return lax.ppermute(values, ("zh", "y", "zl"), pairs)


def qkv_kernel(me_ref, *refs):
    pieces, refs = refs[:TENSOR], refs[TENSOR:]
    gain_ref, weight_ref, cross_ref, q_ref, kv_ref, base_ref, normed, raw, out_rows = refs
    me = me_ref[0]
    rows = raw.shape[0] // TENSOR
    for step in range(TENSOR):
        piece = pieces[step][:rows, :]
        values = piece.astype(F32)
        mean_value = jnp.mean(values, axis=-1, keepdims=True)
        centered = values - mean_value
        variance = jnp.mean(centered * centered, axis=-1, keepdims=True)
        result = centered * lax.rsqrt(variance + EPSILON) * gain_ref[...]
        place = pl.ds(pl.multiple_of(jnp.bitwise_xor(me, step) * rows, rows), rows)
        normed[place, :] = result.astype(BF16)
        raw[place, :] = piece
        share = pieces[step][rows:, :]
        fill = jnp.zeros((SLOT - share.shape[0], share.shape[1]), BF16)
        place = pl.ds(pl.multiple_of(jnp.bitwise_xor(me, step) * SLOT, SLOT), SLOT)
        out_rows[place, :] = jnp.concatenate([share, fill], axis=0)
    x = normed[...]
    width = 2 * EHD
    for part in range(2):
        out = lax.dot_general(weight_ref[1 + part], x, NT, preferred_element_type=F32)
        kv_ref[part * width : (part + 1) * width, :] = out.astype(BF16)
    q = lax.dot_general(x, weight_ref[0], NT, preferred_element_type=F32)
    for head in range(2):
        q_ref[head] = q[:, head * EHD : (head + 1) * EHD].astype(BF16)
    cross = cross_ref[...]
    fold = jnp.dot(out_rows[...], cross, preferred_element_type=F32)
    row = lax.broadcasted_iota(jnp.int32, (TENSOR * SHARE, TENSOR * SLOT), 0)
    column = lax.broadcasted_iota(jnp.int32, (TENSOR * SHARE, TENSOR * SLOT), 1)
    chosen = (column == row + ((row * 3277) >> 16) * (SLOT - SHARE)).astype(F32).astype(BF16)
    fold = jnp.dot(chosen, fold.astype(BF16), preferred_element_type=F32)
    kv_ref[4 * EHD :, :] = fold.astype(BF16)
    base_ref[...] = jnp.dot(raw[...], cross, preferred_element_type=F32)


def encoder_kernel(q_ref, *refs):
    count = 8
    pieces, (out_ref, scores) = refs[:count], refs[count:]
    rows = q_ref.shape[1]
    scale = 1.0 / math.sqrt(EHD)
    for head in range(2):
        q = q_ref[head]
        top = None
        for j in range(count):
            s = jnp.dot(q, pieces[j][head * EHD : (head + 1) * EHD, :], preferred_element_type=F32)
            scores[head, :, j * rows : (j + 1) * rows] = s
            part = jnp.maximum(s[:, :128], s[:, 128:])
            top = part if top is None else jnp.maximum(top, part)
        top = jnp.max(top, axis=-1, keepdims=True)
        mix = jnp.zeros((rows, EHD), F32)
        total = jnp.zeros((rows, 128), F32)
        low = 2 * EHD + head * EHD
        for j in range(count):
            p = jnp.exp((scores[head, :, j * rows : (j + 1) * rows] - top) * scale)
            total = total + (p[:, :128] + p[:, 128:])
            mix = mix + lax.dot_general(
                p.astype(BF16), pieces[j][low : low + EHD, :], NT, preferred_element_type=F32
            )
        attended = mix / jnp.sum(total, axis=-1, keepdims=True)
        out_ref[head * EHD : (head + 1) * EHD, :] = attended.T.astype(BF16)


def fold_kernel(place_ref, *refs):
    pieces, (out_ref, stacked) = refs[:8], refs[8:]
    x, c = place_ref[1], place_ref[2]
    size = TENSOR * SHARE
    for k in range(8):
        owner = jnp.bitwise_xor(c, k // 4) * 4 + jnp.bitwise_xor(x, k % 4)
        low = pl.multiple_of(owner * size, size)
        stacked[pl.ds(low, size), :] = pieces[k][4 * EHD :, :]
    for t in range(TENSOR):
        row = lax.broadcasted_iota(jnp.int32, (size, 8 * size), 0)
        column = lax.broadcasted_iota(jnp.int32, (size, 8 * size), 1)
        owner = (row * 3277) >> 16
        source = owner * (size - SHARE) + row + t * SHARE
        chosen = (column == source).astype(F32).astype(BF16)
        out = jnp.dot(chosen, stacked[...], preferred_element_type=F32)
        out_ref[t] = out.astype(BF16)


def cross_kernel(me_ref, *refs):
    pieces, (weight_ref, base_ref, gain_ref, out_ref) = refs[:TENSOR], refs[TENSOR:]
    me = me_ref[0]
    proj = base_ref[...]
    for step in range(TENSOR):
        weight = weight_ref[jnp.bitwise_xor(me, step)]
        proj = proj + lax.dot_general(
            pieces[step][...], weight, (((0,), (0,)), ((), ())), preferred_element_type=F32
        )
    keys = proj[:, :HD]
    square_mean = jnp.mean(keys * keys, axis=-1, keepdims=True)
    keys = keys * lax.rsqrt(square_mean + EPSILON) * gain_ref[...]
    out_ref[:, :HD] = keys.astype(BF16)
    out_ref[:, HD:] = proj[:, HD:].astype(BF16)


def query_part(x_ref, gain_ref, weights, total, square):
    depth = weights[0].shape[0]
    out, squares = total[...], square[...]
    for k, weight_ref in enumerate(weights):
        columns = slice(k * depth, (k + 1) * depth)
        x = x_ref[:, columns].astype(F32)
        for low in range(0, depth, 128):
            part = x[:, low : low + 128]
            squares = squares + part * part
        scaled = (x * gain_ref[:, columns]).astype(BF16)
        out = out + jnp.dot(scaled, weight_ref[...], preferred_element_type=F32)
    total[...], square[...] = out, squares


def query_first_kernel(x_ref, gain_ref, *refs):
    weights, (total, square) = refs[:STREAMS], refs[STREAMS:]

    @pl.when(pl.program_id(0) == 0)
    def _():
        total[...] = jnp.zeros_like(total)
        square[...] = jnp.zeros_like(square)

    query_part(x_ref, gain_ref, weights, total, square)


def query_last_kernel(width, x_ref, gain_ref, *refs):
    weights, refs = refs[:STREAMS], refs[STREAMS:]
    begun, squares, head_gain_ref, image_ref, count_ref, out_ref, total, square = refs
    rows = x_ref.shape[0]

    @pl.when(pl.program_id(0) == 0)
    def _():
        total[...] = begun[...]
        square[...] = squares[...]

    query_part(x_ref, gain_ref, weights, total, square)

    @pl.when(pl.program_id(0) == pl.num_programs(0) - 1)
    def _():
        inverse = lax.rsqrt(jnp.sum(square[...], axis=-1, keepdims=True) / width + EPSILON)
        for head in range(4):
            q = total[:, head * HD : (head + 1) * HD] * inverse
            mean = jnp.mean(q * q, axis=-1, keepdims=True)
            q = q * lax.rsqrt(mean + EPSILON) * head_gain_ref[...] / math.sqrt(HD)
            out_ref[:rows, head * HD : (head + 1) * HD] = q.astype(BF16)
        count = count_ref[...]
        extra = jnp.concatenate([image_ref[...], count >> 4, count & 15], axis=0)
        extra = jnp.concatenate([extra, jnp.zeros((13, rows), jnp.int32)], axis=0)
        out_ref[rows:, :rows] = extra.astype(F32).astype(BF16)
        out_ref[rows:, rows:] = jnp.zeros((16, out_ref.shape[1] - rows), BF16)


def decode_rows(q, limit, first, slabs):
    keys = slabs[0].shape[0]
    lane = lax.broadcasted_iota(jnp.int32, (1, keys), 1)
    base = ((lane >> 5) & 3) * 512 + (lane >> 7) * 128 + (lane & 31)
    mix = jnp.zeros((q.shape[0], HD), F32)
    total = jnp.zeros((q.shape[0], 128), F32)
    for j in range(8):
        pos = (base + first[j]).astype(F32)
        s = lax.dot_general(q, slabs[j][:, :HD], NT, preferred_element_type=F32)
        w = jnp.where(pos < limit, jnp.exp(s), 0.0)
        total = total + (w[:, :128] + w[:, 128:])
        mix = mix + jnp.dot(w.astype(BF16), slabs[j][:, HD:], preferred_element_type=F32)
    total = jnp.sum(total, axis=-1, keepdims=True)
    return (mix / jnp.where(total > 0.0, total, 1.0)).astype(BF16)


def decode_kernel(place_ref, query_ref, *refs):
    slabs, out_ref = refs[:8], refs[8]
    rows = out_ref.shape[0]
    few = rows // 2
    zh, x, c = place_ref[0], place_ref[1], place_ref[2]
    first = [jnp.bitwise_xor(c, j // 4) * 256 + jnp.bitwise_xor(x, j % 4) * 32 for j in range(8)]
    extra = query_ref[rows : rows + 8, :HD].astype(F32)
    mine = extra[0:1] == zh.astype(F32)
    limit = jnp.where(mine, extra[1:2] * 16.0 + extra[2:3], 0.0)
    member = mine.astype(F32)
    count = jnp.sum(member)

    @pl.when(count <= few)
    def _():
        below = lax.broadcasted_iota(jnp.int32, (rows, rows), 0)
        below = below < lax.broadcasted_iota(jnp.int32, (rows, rows), 1)
        rank = jnp.dot(
            jnp.broadcast_to(member, (8, rows)).astype(BF16),
            below.astype(F32).astype(BF16),
            preferred_element_type=F32,
        )[0:1]
        slot = lax.broadcasted_iota(jnp.int32, (few, rows), 0).astype(F32)
        chosen = jnp.where(rank == slot, member, 0.0)
        picked = chosen.astype(BF16)
        q = jnp.dot(picked, query_ref[:rows, :], preferred_element_type=F32).astype(BF16)
        q = jnp.concatenate([q[:, head * HD : (head + 1) * HD] for head in range(4)], axis=0)
        bound = jnp.sum(chosen * limit, axis=-1, keepdims=True)
        out = decode_rows(q, jnp.concatenate([bound] * 4, axis=0), first, slabs)
        out = jnp.concatenate([out[head * few : (head + 1) * few] for head in range(4)], axis=1)
        back = chosen.T.astype(BF16)
        out_ref[...] = jnp.dot(back, out, preferred_element_type=F32).astype(BF16)

    @pl.when(count > few)
    def _():
        bound = jnp.broadcast_to(limit, (8, rows)).T[:, 0:1]
        q = [query_ref[:rows, head * HD : (head + 1) * HD] for head in range(4)]
        q = jnp.concatenate(q, axis=0)
        out = decode_rows(q, jnp.concatenate([bound] * 4, axis=0), first, slabs)
        for head in range(4):
            out_ref[:, head * HD : (head + 1) * HD] = out[head * rows : (head + 1) * rows]


def limits(mib):
    return pltpu.CompilerParams(vmem_limit_bytes=mib << 20)


def gather_xc(piece):
    along_x = {0: piece}
    for k in X_ORDER:
        along_x[k] = xor_permute(piece, "x", XS, k)
    along_x = [along_x[k] for k in range(XS)]
    return along_x + [xor_permute(value, "c", CORES, 1) for value in along_x]


def gather_tensor(piece):
    pieces = {0: piece}
    for k in TENSOR_ORDER:
        pieces[k] = xor_permute(piece, ("y", "zl"), TENSOR, k)
    return [pieces[k] for k in range(TENSOR)]


def on_device(
    patches,
    enc_gain,
    enc_qkv,
    enc_out,
    cross_kv,
    key_gain,
    dec_hidden,
    dec_gain,
    query_weight,
    query_gain,
    image_of_row,
    valid_count,
):
    tensor_index = (lax.axis_index("y") * ZL + lax.axis_index("zl")).astype(jnp.int32)
    me = tensor_index.reshape(1)
    place = jnp.stack([lax.axis_index("zh"), lax.axis_index("x"), lax.axis_index("c")]).astype(
        jnp.int32
    )
    patch_rows, width = patches.shape
    rows = patch_rows * TENSOR
    own = image_permute(patches)

    dec_rows = dec_hidden.shape[0]
    depth, first_steps, last_steps = 1024, 4, 4
    dec_width, query_width = query_weight.shape
    fixed = lambda shape: pl.BlockSpec(shape, lambda i: (0, 0))
    gain_view = dec_gain.reshape(1, -1)
    weights = [query_weight] * STREAMS

    def weight_blocks(begin):
        shape = (depth // STREAMS, query_width)
        return [
            pl.BlockSpec(shape, lambda i, k=k: ((i + begin) * STREAMS + k, 0))
            for k in range(STREAMS)
        ]

    begun, squares = pl.pallas_call(
        query_first_kernel,
        grid=(first_steps,),
        out_shape=(
            jax.ShapeDtypeStruct((dec_rows, query_width), F32),
            jax.ShapeDtypeStruct((dec_rows, 128), F32),
        ),
        in_specs=[
            pl.BlockSpec((dec_rows, depth), lambda i: (0, i)),
            pl.BlockSpec((1, depth), lambda i: (0, i)),
        ]
        + weight_blocks(0),
        out_specs=(fixed((dec_rows, query_width)), fixed((dec_rows, 128))),
        compiler_params=limits(56),
    )(dec_hidden, gain_view, *weights)
    message = pl.pallas_call(
        functools.partial(query_last_kernel, dec_width),
        grid=(last_steps,),
        out_shape=jax.ShapeDtypeStruct((dec_rows + 16, query_width), BF16),
        in_specs=[
            pl.BlockSpec((dec_rows, depth), lambda i: (0, i + first_steps)),
            pl.BlockSpec((1, depth), lambda i: (0, i + first_steps)),
            *weight_blocks(first_steps),
            fixed((dec_rows, query_width)),
            fixed((dec_rows, 128)),
            fixed((1, HD)),
            fixed((1, dec_rows)),
            fixed((1, dec_rows)),
        ],
        out_specs=fixed((dec_rows + 16, query_width)),
        scratch_shapes=[pltpu.VMEM((dec_rows, query_width), F32), pltpu.VMEM((dec_rows, 128), F32)],
        compiler_params=limits(56),
    )(
        dec_hidden,
        gain_view,
        *weights,
        begun,
        squares,
        query_gain.reshape(1, -1),
        image_of_row.reshape(1, -1),
        valid_count.reshape(1, -1),
    )

    owner = lax.axis_index("c") * XS + lax.axis_index("x")
    share = lax.dynamic_slice_in_dim(enc_out, owner * SHARE, SHARE, axis=0)
    share = jnp.pad(share, ((0, 24 - SHARE), (0, 0)))
    gain_row = enc_gain.reshape(1, -1)
    pieces = gather_tensor(jnp.concatenate([own, share], axis=0))
    q, kv, base = pl.pallas_call(
        qkv_kernel,
        out_shape=(
            jax.ShapeDtypeStruct((2, rows, EHD), BF16),
            jax.ShapeDtypeStruct((4 * EHD + TENSOR * SHARE, rows), BF16),
            jax.ShapeDtypeStruct((rows, 2 * HD), F32),
        ),
        in_specs=[smem()] + vmem(TENSOR + 3),
        out_specs=tuple(vmem(3)),
        scratch_shapes=[
            pltpu.VMEM((rows, width), BF16),
            pltpu.VMEM((rows, width), BF16),
            pltpu.VMEM((TENSOR * SLOT, width), BF16),
        ],
        compiler_params=limits(16),
    )(me, *pieces, gain_row, enc_qkv.transpose(0, 2, 1), cross_kv)
    kv_pieces = gather_xc(kv)
    every_query = [message]
    for k in range(1, ZH):
        every_query.append(xor_permute(message, "zh", ZH, k))

    attended = pl.pallas_call(
        encoder_kernel,
        out_shape=jax.ShapeDtypeStruct((2 * EHD, rows), BF16),
        in_specs=vmem(9),
        out_specs=vmem(1)[0],
        scratch_shapes=[pltpu.VMEM((2, rows, 8 * rows), F32)],
        compiler_params=limits(20),
    )(q, *kv_pieces)
    attended_pieces = gather_tensor(attended)
    folded = pl.pallas_call(
        fold_kernel,
        out_shape=jax.ShapeDtypeStruct((TENSOR, 2 * EHD, 2 * HD), BF16),
        in_specs=[smem()] + vmem(8),
        out_specs=vmem(1)[0],
        scratch_shapes=[pltpu.VMEM((TENSOR * 2 * EHD, 2 * HD), BF16)],
        compiler_params=limits(16),
    )(place, *kv_pieces)
    slab = pl.pallas_call(
        cross_kernel,
        out_shape=jax.ShapeDtypeStruct((rows, 2 * HD), BF16),
        in_specs=[smem()] + vmem(TENSOR + 3),
        out_specs=vmem(1)[0],
        compiler_params=limits(12),
    )(me, *attended_pieces, folded, base, key_gain.reshape(1, -1))
    slabs = gather_xc(slab)
    result = None
    for k in (2, 1, 3, 0):
        out = pl.pallas_call(
            decode_kernel,
            out_shape=jax.ShapeDtypeStruct((dec_rows, 4 * HD), BF16),
            in_specs=[smem()] + vmem(9),
            out_specs=vmem(1)[0],
            compiler_params=limits(12),
        )(place, every_query[k], *slabs)
        if k:
            out = xor_permute(out, "zh", ZH, k)
        result = out if result is None else result + out
    return result


def solution(mesh):
    parts = Mesh(mesh.devices.reshape(ZH, CORES, YS, ZL, XS), ("zh", "c", "y", "zl", "x"))
    group, tensor, seq = ("zh", "c"), ("y", "zl"), ("x",)
    in_specs = (
        P(group + tensor + seq, None),
        P(),
        P(None, None, tensor),
        P(tensor, None),
        P(None, tensor),
        P(),
        P(group + seq, None),
        P(),
        P(None, tensor),
        P(),
        P(group + seq),
        P(group + seq),
    )
    out_specs = P(group + seq, tensor)

    return jax.shard_map(
        on_device, mesh=parts, in_specs=in_specs, out_specs=out_specs, check_vma=False
    )
```

```python
import functools
import math

import jax
import jax.numpy as jnp
from jax import lax
from jax.experimental import pallas as pl
from jax.experimental.pallas import tpu as pltpu
from jax.sharding import Mesh
from jax.sharding import PartitionSpec as P

EHD = 80
HD = 128
EPSILON = 1e-05
F32 = jnp.float32
BF16 = jnp.bfloat16
ZH, CORES, YS, ZL, XS = 4, 2, 4, 2, 4
SHARE, SLOT, STREAMS = 20, 32, 4
TENSOR_ORDER, X_ORDER = (5, 7, 3, 4, 6, 2, 1), (2, 3, 1)
TENSOR = YS * ZL
NT = (((1,), (1,)), ((), ()))


def vmem(count):
    return [pl.BlockSpec(memory_space=pltpu.VMEM)] * count


def smem():
    return pl.BlockSpec(memory_space=pltpu.SMEM)


def xor_permute(values, axes, size, step):
    return lax.ppermute(values, axes, [(i, i ^ step) for i in range(size)])


def image_permute(values):
    pairs = []
    for zh in range(ZH):
        for y in range(YS):
            for zl in range(ZL):
                image, slot = (y % 2) * 2 + zl, (y // 2) * ZH + zh
                pairs.append(((zh * YS + y) * ZL + zl, image * TENSOR + slot))
    return lax.ppermute(values, ("zh", "y", "zl"), pairs)


def qkv_kernel(me_ref, *refs):
    pieces, refs = refs[:TENSOR], refs[TENSOR:]
    gain_ref, weight_ref, cross_ref, kv_ref, normed, raw, out_rows = refs
    me = me_ref[0]
    rows = raw.shape[0] // TENSOR
    for step in range(TENSOR):
        piece = pieces[step][:rows, :]
        values = piece.astype(F32)
        mean_value = jnp.mean(values, axis=-1, keepdims=True)
        centered = values - mean_value
        variance = jnp.mean(centered * centered, axis=-1, keepdims=True)
        result = centered * lax.rsqrt(variance + EPSILON) * gain_ref[...]
        place = pl.ds(pl.multiple_of(jnp.bitwise_xor(me, step) * rows, rows), rows)
        normed[place, :] = result.astype(BF16)
        raw[place, :] = piece
        share = pieces[step][rows:, :]
        fill = jnp.zeros((SLOT - share.shape[0], share.shape[1]), BF16)
        place = pl.ds(pl.multiple_of(jnp.bitwise_xor(me, step) * SLOT, SLOT), SLOT)
        out_rows[place, :] = jnp.concatenate([share, fill], axis=0)
    x = normed[...]
    width = 2 * EHD
    for part in range(2):
        out = lax.dot_general(weight_ref[1 + part], x, NT, preferred_element_type=F32)
        kv_ref[part * width : (part + 1) * width, :] = out.astype(BF16)
    fold = jnp.dot(out_rows[...], cross_ref[...], preferred_element_type=F32)
    row = lax.broadcasted_iota(jnp.int32, (TENSOR * SHARE, TENSOR * SLOT), 0)
    column = lax.broadcasted_iota(jnp.int32, (TENSOR * SHARE, TENSOR * SLOT), 1)
    chosen = (column == row + ((row * 3277) >> 16) * (SLOT - SHARE)).astype(F32).astype(BF16)
    fold = jnp.dot(chosen, fold.astype(BF16), preferred_element_type=F32)
    kv_ref[4 * EHD :, :] = fold.astype(BF16)


def local_kernel(normed_ref, raw_ref, weight_ref, cross_ref, q_ref, base_ref):
    q = lax.dot_general(normed_ref[...], weight_ref[0], NT, preferred_element_type=F32)
    for head in range(2):
        q_ref[head] = q[:, head * EHD : (head + 1) * EHD].astype(BF16)
    base_ref[...] = jnp.dot(raw_ref[...], cross_ref[...], preferred_element_type=F32)


def encoder_kernel(q_ref, *refs):
    count = 8
    pieces, (out_ref, scores) = refs[:count], refs[count:]
    rows = q_ref.shape[1]
    scale = 1.0 / math.sqrt(EHD)
    for head in range(2):
        q = q_ref[head]
        top = None
        for j in range(count):
            s = jnp.dot(q, pieces[j][head * EHD : (head + 1) * EHD, :], preferred_element_type=F32)
            scores[head, :, j * rows : (j + 1) * rows] = s
            part = jnp.maximum(s[:, :128], s[:, 128:])
            top = part if top is None else jnp.maximum(top, part)
        top = jnp.max(top, axis=-1, keepdims=True)
        mix = jnp.zeros((rows, EHD), F32)
        total = jnp.zeros((rows, 128), F32)
        low = 2 * EHD + head * EHD
        for j in range(count):
            p = jnp.exp((scores[head, :, j * rows : (j + 1) * rows] - top) * scale)
            total = total + (p[:, :128] + p[:, 128:])
            mix = mix + lax.dot_general(
                p.astype(BF16), pieces[j][low : low + EHD, :], NT, preferred_element_type=F32
            )
        attended = mix / jnp.sum(total, axis=-1, keepdims=True)
        out_ref[head * EHD : (head + 1) * EHD, :] = attended.T.astype(BF16)


def fold_kernel(place_ref, *refs):
    pieces, (out_ref, stacked) = refs[:8], refs[8:]
    x, c = place_ref[1], place_ref[2]
    size = TENSOR * SHARE
    for k in range(8):
        owner = jnp.bitwise_xor(c, k // 4) * 4 + jnp.bitwise_xor(x, k % 4)
        low = pl.multiple_of(owner * size, size)
        stacked[pl.ds(low, size), :] = pieces[k][4 * EHD :, :]
    for t in range(TENSOR):
        row = lax.broadcasted_iota(jnp.int32, (size, 8 * size), 0)
        column = lax.broadcasted_iota(jnp.int32, (size, 8 * size), 1)
        owner = (row * 3277) >> 16
        source = owner * (size - SHARE) + row + t * SHARE
        chosen = (column == source).astype(F32).astype(BF16)
        out = jnp.dot(chosen, stacked[...], preferred_element_type=F32)
        out_ref[t] = out.astype(BF16)


def cross_kernel(me_ref, *refs):
    pieces, (weight_ref, base_ref, gain_ref, out_ref) = refs[:TENSOR], refs[TENSOR:]
    me = me_ref[0]
    proj = base_ref[...]
    for step in range(TENSOR):
        weight = weight_ref[jnp.bitwise_xor(me, step)]
        proj = proj + lax.dot_general(
            pieces[step][...], weight, (((0,), (0,)), ((), ())), preferred_element_type=F32
        )
    keys = proj[:, :HD]
    square_mean = jnp.mean(keys * keys, axis=-1, keepdims=True)
    keys = keys * lax.rsqrt(square_mean + EPSILON) * gain_ref[...]
    out_ref[:, :HD] = keys.astype(BF16)
    out_ref[:, HD:] = proj[:, HD:].astype(BF16)


def query_part(x_ref, gain_ref, weights, total, square):
    depth = weights[0].shape[0]
    out, squares = total[...], square[...]
    for k, weight_ref in enumerate(weights):
        columns = slice(k * depth, (k + 1) * depth)
        x = x_ref[:, columns].astype(F32)
        for low in range(0, depth, 128):
            part = x[:, low : low + 128]
            squares = squares + part * part
        scaled = (x * gain_ref[:, columns]).astype(BF16)
        out = out + jnp.dot(scaled, weight_ref[...], preferred_element_type=F32)
    total[...], square[...] = out, squares


def query_first_kernel(x_ref, gain_ref, *refs):
    weights, (total, square) = refs[:STREAMS], refs[STREAMS:]

    @pl.when(pl.program_id(0) == 0)
    def _():
        total[...] = jnp.zeros_like(total)
        square[...] = jnp.zeros_like(square)

    query_part(x_ref, gain_ref, weights, total, square)


def query_last_kernel(width, x_ref, gain_ref, *refs):
    weights, refs = refs[:STREAMS], refs[STREAMS:]
    begun, squares, head_gain_ref, image_ref, count_ref, out_ref, total, square = refs
    rows = x_ref.shape[0]

    @pl.when(pl.program_id(0) == 0)
    def _():
        total[...] = begun[...]
        square[...] = squares[...]

    query_part(x_ref, gain_ref, weights, total, square)

    @pl.when(pl.program_id(0) == pl.num_programs(0) - 1)
    def _():
        inverse = lax.rsqrt(jnp.sum(square[...], axis=-1, keepdims=True) / width + EPSILON)
        for head in range(4):
            q = total[:, head * HD : (head + 1) * HD] * inverse
            mean = jnp.mean(q * q, axis=-1, keepdims=True)
            q = q * lax.rsqrt(mean + EPSILON) * head_gain_ref[...] / math.sqrt(HD)
            out_ref[:rows, head * HD : (head + 1) * HD] = q.astype(BF16)
        count = count_ref[...]
        extra = jnp.concatenate([image_ref[...], count >> 4, count & 15], axis=0)
        extra = jnp.concatenate([extra, jnp.zeros((13, rows), jnp.int32)], axis=0)
        out_ref[rows:, :rows] = extra.astype(F32).astype(BF16)
        out_ref[rows:, rows:] = jnp.zeros((16, out_ref.shape[1] - rows), BF16)


def decode_rows(q, limit, first, slabs):
    keys = slabs[0].shape[0]
    lane = lax.broadcasted_iota(jnp.int32, (1, keys), 1)
    base = ((lane >> 5) & 3) * 512 + (lane >> 7) * 128 + (lane & 31)
    mix = jnp.zeros((q.shape[0], HD), F32)
    total = jnp.zeros((q.shape[0], 128), F32)
    for j in range(8):
        pos = (base + first[j]).astype(F32)
        s = lax.dot_general(q, slabs[j][:, :HD], NT, preferred_element_type=F32)
        w = jnp.where(pos < limit, jnp.exp(s), 0.0)
        total = total + (w[:, :128] + w[:, 128:])
        mix = mix + jnp.dot(w.astype(BF16), slabs[j][:, HD:], preferred_element_type=F32)
    total = jnp.sum(total, axis=-1, keepdims=True)
    return (mix / jnp.where(total > 0.0, total, 1.0)).astype(BF16)


def decode_kernel(place_ref, query_ref, *refs):
    slabs, out_ref = refs[:8], refs[8]
    rows = out_ref.shape[0]
    few = rows // 2
    zh, x, c = place_ref[0], place_ref[1], place_ref[2]
    first = [jnp.bitwise_xor(c, j // 4) * 256 + jnp.bitwise_xor(x, j % 4) * 32 for j in range(8)]
    extra = query_ref[rows : rows + 8, :HD].astype(F32)
    mine = extra[0:1] == zh.astype(F32)
    limit = jnp.where(mine, extra[1:2] * 16.0 + extra[2:3], 0.0)
    member = mine.astype(F32)
    count = jnp.sum(member)

    @pl.when(count <= few)
    def _():
        below = lax.broadcasted_iota(jnp.int32, (rows, rows), 0)
        below = below < lax.broadcasted_iota(jnp.int32, (rows, rows), 1)
        rank = jnp.dot(
            jnp.broadcast_to(member, (8, rows)).astype(BF16),
            below.astype(F32).astype(BF16),
            preferred_element_type=F32,
        )[0:1]
        slot = lax.broadcasted_iota(jnp.int32, (few, rows), 0).astype(F32)
        chosen = jnp.where(rank == slot, member, 0.0)
        picked = chosen.astype(BF16)
        q = jnp.dot(picked, query_ref[:rows, :], preferred_element_type=F32).astype(BF16)
        q = jnp.concatenate([q[:, head * HD : (head + 1) * HD] for head in range(4)], axis=0)
        bound = jnp.sum(chosen * limit, axis=-1, keepdims=True)
        out = decode_rows(q, jnp.concatenate([bound] * 4, axis=0), first, slabs)
        out = jnp.concatenate([out[head * few : (head + 1) * few] for head in range(4)], axis=1)
        back = chosen.T.astype(BF16)
        out_ref[...] = jnp.dot(back, out, preferred_element_type=F32).astype(BF16)

    @pl.when(count > few)
    def _():
        bound = jnp.broadcast_to(limit, (8, rows)).T[:, 0:1]
        q = [query_ref[:rows, head * HD : (head + 1) * HD] for head in range(4)]
        q = jnp.concatenate(q, axis=0)
        out = decode_rows(q, jnp.concatenate([bound] * 4, axis=0), first, slabs)
        for head in range(4):
            out_ref[:, head * HD : (head + 1) * HD] = out[head * rows : (head + 1) * rows]


def limits(mib):
    return pltpu.CompilerParams(vmem_limit_bytes=mib << 20)


def gather_xc(piece):
    along_x = {0: piece}
    for k in X_ORDER:
        along_x[k] = xor_permute(piece, "x", XS, k)
    along_x = [along_x[k] for k in range(XS)]
    return along_x + [xor_permute(value, "c", CORES, 1) for value in along_x]


def gather_tensor(piece):
    pieces = {0: piece}
    for k in TENSOR_ORDER:
        pieces[k] = xor_permute(piece, ("y", "zl"), TENSOR, k)
    return [pieces[k] for k in range(TENSOR)]


def on_device(
    patches,
    enc_gain,
    enc_qkv,
    enc_out,
    cross_kv,
    key_gain,
    dec_hidden,
    dec_gain,
    query_weight,
    query_gain,
    image_of_row,
    valid_count,
):
    tensor_index = (lax.axis_index("y") * ZL + lax.axis_index("zl")).astype(jnp.int32)
    me = tensor_index.reshape(1)
    place = jnp.stack([lax.axis_index("zh"), lax.axis_index("x"), lax.axis_index("c")]).astype(
        jnp.int32
    )
    patch_rows, width = patches.shape
    rows = patch_rows * TENSOR
    own = image_permute(patches)

    dec_rows = dec_hidden.shape[0]
    depth, first_steps, last_steps = 1024, 4, 4
    dec_width, query_width = query_weight.shape
    fixed = lambda shape: pl.BlockSpec(shape, lambda i: (0, 0))
    gain_view = dec_gain.reshape(1, -1)
    weights = [query_weight] * STREAMS

    def weight_blocks(begin):
        shape = (depth // STREAMS, query_width)
        return [
            pl.BlockSpec(shape, lambda i, k=k: ((i + begin) * STREAMS + k, 0))
            for k in range(STREAMS)
        ]

    begun, squares = pl.pallas_call(
        query_first_kernel,
        grid=(first_steps,),
        out_shape=(
            jax.ShapeDtypeStruct((dec_rows, query_width), F32),
            jax.ShapeDtypeStruct((dec_rows, 128), F32),
        ),
        in_specs=[
            pl.BlockSpec((dec_rows, depth), lambda i: (0, i)),
            pl.BlockSpec((1, depth), lambda i: (0, i)),
        ]
        + weight_blocks(0),
        out_specs=(fixed((dec_rows, query_width)), fixed((dec_rows, 128))),
        compiler_params=limits(56),
    )(dec_hidden, gain_view, *weights)
    message = pl.pallas_call(
        functools.partial(query_last_kernel, dec_width),
        grid=(last_steps,),
        out_shape=jax.ShapeDtypeStruct((dec_rows + 16, query_width), BF16),
        in_specs=[
            pl.BlockSpec((dec_rows, depth), lambda i: (0, i + first_steps)),
            pl.BlockSpec((1, depth), lambda i: (0, i + first_steps)),
            *weight_blocks(first_steps),
            fixed((dec_rows, query_width)),
            fixed((dec_rows, 128)),
            fixed((1, HD)),
            fixed((1, dec_rows)),
            fixed((1, dec_rows)),
        ],
        out_specs=fixed((dec_rows + 16, query_width)),
        scratch_shapes=[pltpu.VMEM((dec_rows, query_width), F32), pltpu.VMEM((dec_rows, 128), F32)],
        compiler_params=limits(56),
    )(
        dec_hidden,
        gain_view,
        *weights,
        begun,
        squares,
        query_gain.reshape(1, -1),
        image_of_row.reshape(1, -1),
        valid_count.reshape(1, -1),
    )

    owner = lax.axis_index("c") * XS + lax.axis_index("x")
    share = lax.dynamic_slice_in_dim(enc_out, owner * SHARE, SHARE, axis=0)
    share = jnp.pad(share, ((0, 24 - SHARE), (0, 0)))
    gain_row = enc_gain.reshape(1, -1)
    pieces = gather_tensor(jnp.concatenate([own, share], axis=0))
    qkv_weight = enc_qkv.transpose(0, 2, 1)
    row_shape = jax.ShapeDtypeStruct((rows, width), BF16)
    kv, normed, raw = pl.pallas_call(
        qkv_kernel,
        out_shape=(
            jax.ShapeDtypeStruct((4 * EHD + TENSOR * SHARE, rows), BF16),
            row_shape,
            row_shape,
        ),
        in_specs=[smem()] + vmem(TENSOR + 3),
        out_specs=tuple(vmem(3)),
        scratch_shapes=[pltpu.VMEM((TENSOR * SLOT, width), BF16)],
        compiler_params=limits(16),
    )(me, *pieces, gain_row, qkv_weight, cross_kv)
    kv_pieces = gather_xc(kv)
    q, base = pl.pallas_call(
        local_kernel,
        out_shape=(
            jax.ShapeDtypeStruct((2, rows, EHD), BF16),
            jax.ShapeDtypeStruct((rows, 2 * HD), F32),
        ),
        in_specs=vmem(4),
        out_specs=tuple(vmem(2)),
        compiler_params=limits(12),
    )(normed, raw, qkv_weight, cross_kv)
    every_query = [message]
    for k in range(1, ZH):
        every_query.append(xor_permute(message, "zh", ZH, k))

    attended = pl.pallas_call(
        encoder_kernel,
        out_shape=jax.ShapeDtypeStruct((2 * EHD, rows), BF16),
        in_specs=vmem(9),
        out_specs=vmem(1)[0],
        scratch_shapes=[pltpu.VMEM((2, rows, 8 * rows), F32)],
        compiler_params=limits(20),
    )(q, *kv_pieces)
    attended_pieces = gather_tensor(attended)
    folded = pl.pallas_call(
        fold_kernel,
        out_shape=jax.ShapeDtypeStruct((TENSOR, 2 * EHD, 2 * HD), BF16),
        in_specs=[smem()] + vmem(8),
        out_specs=vmem(1)[0],
        scratch_shapes=[pltpu.VMEM((TENSOR * 2 * EHD, 2 * HD), BF16)],
        compiler_params=limits(16),
    )(place, *kv_pieces)
    slab = pl.pallas_call(
        cross_kernel,
        out_shape=jax.ShapeDtypeStruct((rows, 2 * HD), BF16),
        in_specs=[smem()] + vmem(TENSOR + 3),
        out_specs=vmem(1)[0],
        compiler_params=limits(12),
    )(me, *attended_pieces, folded, base, key_gain.reshape(1, -1))
    slabs = gather_xc(slab)
    result = None
    for k in (2, 1, 3, 0):
        out = pl.pallas_call(
            decode_kernel,
            out_shape=jax.ShapeDtypeStruct((dec_rows, 4 * HD), BF16),
            in_specs=[smem()] + vmem(9),
            out_specs=vmem(1)[0],
            compiler_params=limits(12),
        )(place, every_query[k], *slabs)
        if k:
            out = xor_permute(out, "zh", ZH, k)
        result = out if result is None else result + out
    return result


def solution(mesh):
    parts = Mesh(mesh.devices.reshape(ZH, CORES, YS, ZL, XS), ("zh", "c", "y", "zl", "x"))
    group, tensor, seq = ("zh", "c"), ("y", "zl"), ("x",)
    in_specs = (
        P(group + tensor + seq, None),
        P(),
        P(None, None, tensor),
        P(tensor, None),
        P(None, tensor),
        P(),
        P(group + seq, None),
        P(),
        P(None, tensor),
        P(),
        P(group + seq),
        P(group + seq),
    )
    out_specs = P(group + seq, tensor)

    return jax.shard_map(
        on_device, mesh=parts, in_specs=in_specs, out_specs=out_specs, check_vma=False
    )
```

```python
import functools
import math

import jax
import jax.numpy as jnp
from jax import lax
from jax.experimental import pallas as pl
from jax.experimental.pallas import tpu as pltpu
from jax.sharding import Mesh
from jax.sharding import PartitionSpec as P

EHD = 80
HD = 128
EPSILON = 1e-05
F32 = jnp.float32
BF16 = jnp.bfloat16
ZH, CORES, YS, ZL, XS = 4, 2, 4, 2, 4
SHARE, SLOT, STREAMS = 20, 32, 4
TENSOR_ORDER, X_ORDER = (5, 7, 3, 4, 6, 2, 1), (2, 3, 1)
TENSOR = YS * ZL
NT = (((1,), (1,)), ((), ()))


def vmem(count):
    return [pl.BlockSpec(memory_space=pltpu.VMEM)] * count


def smem():
    return pl.BlockSpec(memory_space=pltpu.SMEM)


def xor_permute(values, axes, size, step):
    return lax.ppermute(values, axes, [(i, i ^ step) for i in range(size)])


def image_permute(values):
    pairs = []
    for zh in range(ZH):
        for y in range(YS):
            for zl in range(ZL):
                image, slot = (y % 2) * 2 + zl, (y // 2) * ZH + zh
                pairs.append(((zh * YS + y) * ZL + zl, image * TENSOR + slot))
    return lax.ppermute(values, ("zh", "y", "zl"), pairs)


def qkv_kernel(me_ref, *refs):
    pieces, refs = refs[:TENSOR], refs[TENSOR:]
    gain_ref, weight_ref, cross_ref, kv_ref, fold_ref, normed, raw, out_rows = refs
    me = me_ref[0]
    rows = raw.shape[0] // TENSOR
    for step in range(TENSOR):
        piece = pieces[step][:rows, :]
        values = piece.astype(F32)
        mean_value = jnp.mean(values, axis=-1, keepdims=True)
        centered = values - mean_value
        variance = jnp.mean(centered * centered, axis=-1, keepdims=True)
        result = centered * lax.rsqrt(variance + EPSILON) * gain_ref[...]
        place = pl.ds(pl.multiple_of(jnp.bitwise_xor(me, step) * rows, rows), rows)
        normed[place, :] = result.astype(BF16)
        raw[place, :] = piece
        share = pieces[step][rows:, :]
        fill = jnp.zeros((SLOT - share.shape[0], share.shape[1]), BF16)
        place = pl.ds(pl.multiple_of(jnp.bitwise_xor(me, step) * SLOT, SLOT), SLOT)
        out_rows[place, :] = jnp.concatenate([share, fill], axis=0)
    x = normed[...]
    width = 2 * EHD
    for part in range(2):
        out = lax.dot_general(weight_ref[1 + part], x, NT, preferred_element_type=F32)
        kv_ref[part * width : (part + 1) * width, :] = out.astype(BF16)
    fold = jnp.dot(out_rows[...], cross_ref[...], preferred_element_type=F32)
    row = lax.broadcasted_iota(jnp.int32, (TENSOR * SHARE, TENSOR * SLOT), 0)
    column = lax.broadcasted_iota(jnp.int32, (TENSOR * SHARE, TENSOR * SLOT), 1)
    chosen = (column == row + ((row * 3277) >> 16) * (SLOT - SHARE)).astype(F32).astype(BF16)
    fold = jnp.dot(chosen, fold.astype(BF16), preferred_element_type=F32)
    fold_ref[...] = fold.astype(BF16)


def local_kernel(normed_ref, raw_ref, weight_ref, cross_ref, q_ref, base_ref):
    q = lax.dot_general(normed_ref[...], weight_ref[0], NT, preferred_element_type=F32)
    for head in range(2):
        q_ref[head] = q[:, head * EHD : (head + 1) * EHD].astype(BF16)
    base_ref[...] = jnp.dot(raw_ref[...], cross_ref[...], preferred_element_type=F32)


def encoder_kernel(q_ref, *refs):
    count = 8
    pieces, (out_ref, scores) = refs[:count], refs[count:]
    rows = q_ref.shape[1]
    scale = 1.0 / math.sqrt(EHD)
    for head in range(2):
        q = q_ref[head]
        top = None
        for j in range(count):
            s = jnp.dot(q, pieces[j][head * EHD : (head + 1) * EHD, :], preferred_element_type=F32)
            scores[head, :, j * rows : (j + 1) * rows] = s
            part = jnp.maximum(s[:, :128], s[:, 128:])
            top = part if top is None else jnp.maximum(top, part)
        top = jnp.max(top, axis=-1, keepdims=True)
        mix = jnp.zeros((rows, EHD), F32)
        total = jnp.zeros((rows, 128), F32)
        low = 2 * EHD + head * EHD
        for j in range(count):
            p = jnp.exp((scores[head, :, j * rows : (j + 1) * rows] - top) * scale)
            total = total + (p[:, :128] + p[:, 128:])
            mix = mix + lax.dot_general(
                p.astype(BF16), pieces[j][low : low + EHD, :], NT, preferred_element_type=F32
            )
        attended = mix / jnp.sum(total, axis=-1, keepdims=True)
        out_ref[head * EHD : (head + 1) * EHD, :] = attended.T.astype(BF16)


def fold_kernel(place_ref, *refs):
    pieces, (out_ref, stacked) = refs[:8], refs[8:]
    x, c = place_ref[1], place_ref[2]
    size = TENSOR * SHARE
    for k in range(8):
        owner = jnp.bitwise_xor(c, k // 4) * 4 + jnp.bitwise_xor(x, k % 4)
        low = pl.multiple_of(owner * size, size)
        stacked[pl.ds(low, size), :] = pieces[k][...]
    for t in range(TENSOR):
        row = lax.broadcasted_iota(jnp.int32, (size, 8 * size), 0)
        column = lax.broadcasted_iota(jnp.int32, (size, 8 * size), 1)
        owner = (row * 3277) >> 16
        source = owner * (size - SHARE) + row + t * SHARE
        chosen = (column == source).astype(F32).astype(BF16)
        out = jnp.dot(chosen, stacked[...], preferred_element_type=F32)
        out_ref[t] = out.astype(BF16)


def cross_kernel(me_ref, *refs):
    pieces, (weight_ref, base_ref, gain_ref, out_ref) = refs[:TENSOR], refs[TENSOR:]
    me = me_ref[0]
    proj = base_ref[...]
    for step in range(TENSOR):
        weight = weight_ref[jnp.bitwise_xor(me, step)]
        proj = proj + lax.dot_general(
            pieces[step][...], weight, (((0,), (0,)), ((), ())), preferred_element_type=F32
        )
    keys = proj[:, :HD]
    square_mean = jnp.mean(keys * keys, axis=-1, keepdims=True)
    keys = keys * lax.rsqrt(square_mean + EPSILON) * gain_ref[...]
    out_ref[:, :HD] = keys.astype(BF16)
    out_ref[:, HD:] = proj[:, HD:].astype(BF16)


def query_part(x_ref, gain_ref, weights, total, square):
    depth = weights[0].shape[0]
    out, squares = total[...], square[...]
    for k, weight_ref in enumerate(weights):
        columns = slice(k * depth, (k + 1) * depth)
        x = x_ref[:, columns].astype(F32)
        for low in range(0, depth, 128):
            part = x[:, low : low + 128]
            squares = squares + part * part
        scaled = (x * gain_ref[:, columns]).astype(BF16)
        out = out + jnp.dot(scaled, weight_ref[...], preferred_element_type=F32)
    total[...], square[...] = out, squares


def query_first_kernel(x_ref, gain_ref, *refs):
    weights, (total, square) = refs[:STREAMS], refs[STREAMS:]

    @pl.when(pl.program_id(0) == 0)
    def _():
        total[...] = jnp.zeros_like(total)
        square[...] = jnp.zeros_like(square)

    query_part(x_ref, gain_ref, weights, total, square)


def query_last_kernel(width, x_ref, gain_ref, *refs):
    weights, refs = refs[:STREAMS], refs[STREAMS:]
    begun, squares, head_gain_ref, image_ref, count_ref, out_ref, total, square = refs
    rows = x_ref.shape[0]

    @pl.when(pl.program_id(0) == 0)
    def _():
        total[...] = begun[...]
        square[...] = squares[...]

    query_part(x_ref, gain_ref, weights, total, square)

    @pl.when(pl.program_id(0) == pl.num_programs(0) - 1)
    def _():
        inverse = lax.rsqrt(jnp.sum(square[...], axis=-1, keepdims=True) / width + EPSILON)
        for head in range(4):
            q = total[:, head * HD : (head + 1) * HD] * inverse
            mean = jnp.mean(q * q, axis=-1, keepdims=True)
            q = q * lax.rsqrt(mean + EPSILON) * head_gain_ref[...] / math.sqrt(HD)
            out_ref[:rows, head * HD : (head + 1) * HD] = q.astype(BF16)
        count = count_ref[...]
        extra = jnp.concatenate([image_ref[...], count >> 4, count & 15], axis=0)
        extra = jnp.concatenate([extra, jnp.zeros((13, rows), jnp.int32)], axis=0)
        out_ref[rows:, :rows] = extra.astype(F32).astype(BF16)
        out_ref[rows:, rows:] = jnp.zeros((16, out_ref.shape[1] - rows), BF16)


def decode_rows(q, limit, first, slabs):
    keys = slabs[0].shape[0]
    lane = lax.broadcasted_iota(jnp.int32, (1, keys), 1)
    base = ((lane >> 5) & 3) * 512 + (lane >> 7) * 128 + (lane & 31)
    mix = jnp.zeros((q.shape[0], HD), F32)
    total = jnp.zeros((q.shape[0], 128), F32)
    for j in range(8):
        pos = (base + first[j]).astype(F32)
        s = lax.dot_general(q, slabs[j][:, :HD], NT, preferred_element_type=F32)
        w = jnp.where(pos < limit, jnp.exp(s), 0.0)
        total = total + (w[:, :128] + w[:, 128:])
        mix = mix + jnp.dot(w.astype(BF16), slabs[j][:, HD:], preferred_element_type=F32)
    total = jnp.sum(total, axis=-1, keepdims=True)
    return (mix / jnp.where(total > 0.0, total, 1.0)).astype(BF16)


def decode_kernel(place_ref, query_ref, *refs):
    slabs, out_ref = refs[:8], refs[8]
    rows = out_ref.shape[0]
    few = rows // 2
    zh, x, c = place_ref[0], place_ref[1], place_ref[2]
    first = [jnp.bitwise_xor(c, j // 4) * 256 + jnp.bitwise_xor(x, j % 4) * 32 for j in range(8)]
    extra = query_ref[rows : rows + 8, :HD].astype(F32)
    mine = extra[0:1] == zh.astype(F32)
    limit = jnp.where(mine, extra[1:2] * 16.0 + extra[2:3], 0.0)
    member = mine.astype(F32)
    count = jnp.sum(member)

    below = lax.broadcasted_iota(jnp.int32, (rows, rows), 0)
    below = below < lax.broadcasted_iota(jnp.int32, (rows, rows), 1)
    rank = jnp.dot(
        jnp.broadcast_to(member, (8, rows)).astype(BF16),
        below.astype(F32).astype(BF16),
        preferred_element_type=F32,
    )[0:1]
    out_ref[...] = jnp.zeros_like(out_ref)

    def half(step, carry):
        slot = lax.broadcasted_iota(jnp.int32, (few, rows), 0) + step * few
        chosen = jnp.where(rank == slot.astype(F32), member, 0.0)
        picked = chosen.astype(BF16)
        q = jnp.dot(picked, query_ref[:rows, :], preferred_element_type=F32).astype(BF16)
        q = jnp.concatenate([q[:, head * HD : (head + 1) * HD] for head in range(4)], axis=0)
        bound = jnp.sum(chosen * limit, axis=-1, keepdims=True)
        out = decode_rows(q, jnp.concatenate([bound] * 4, axis=0), first, slabs)
        out = jnp.concatenate([out[head * few : (head + 1) * few] for head in range(4)], axis=1)
        back = jnp.dot(chosen.T.astype(BF16), out, preferred_element_type=F32)
        out_ref[...] = (out_ref[...].astype(F32) + back).astype(BF16)
        return carry

    lax.fori_loop(0, jnp.where(count > few, 2, 1), half, 0)


def limits(mib):
    return pltpu.CompilerParams(vmem_limit_bytes=mib << 20)


def gather_xc(piece):
    along_x = {0: piece}
    for k in X_ORDER:
        along_x[k] = xor_permute(piece, "x", XS, k)
    along_x = [along_x[k] for k in range(XS)]
    return along_x + [xor_permute(value, "c", CORES, 1) for value in along_x]


def gather_tensor(piece):
    pieces = {0: piece}
    for k in TENSOR_ORDER:
        pieces[k] = xor_permute(piece, ("y", "zl"), TENSOR, k)
    return [pieces[k] for k in range(TENSOR)]


def on_device(
    patches,
    enc_gain,
    enc_qkv,
    enc_out,
    cross_kv,
    key_gain,
    dec_hidden,
    dec_gain,
    query_weight,
    query_gain,
    image_of_row,
    valid_count,
):
    tensor_index = (lax.axis_index("y") * ZL + lax.axis_index("zl")).astype(jnp.int32)
    me = tensor_index.reshape(1)
    place = jnp.stack([lax.axis_index("zh"), lax.axis_index("x"), lax.axis_index("c")]).astype(
        jnp.int32
    )
    patch_rows, width = patches.shape
    rows = patch_rows * TENSOR
    own = image_permute(patches)

    dec_rows = dec_hidden.shape[0]
    depth, first_steps, last_steps = 1024, 4, 4
    dec_width, query_width = query_weight.shape
    fixed = lambda shape: pl.BlockSpec(shape, lambda i: (0, 0))
    gain_view = dec_gain.reshape(1, -1)
    weights = [query_weight] * STREAMS

    def weight_blocks(begin):
        shape = (depth // STREAMS, query_width)
        return [
            pl.BlockSpec(shape, lambda i, k=k: ((i + begin) * STREAMS + k, 0))
            for k in range(STREAMS)
        ]

    begun, squares = pl.pallas_call(
        query_first_kernel,
        grid=(first_steps,),
        out_shape=(
            jax.ShapeDtypeStruct((dec_rows, query_width), F32),
            jax.ShapeDtypeStruct((dec_rows, 128), F32),
        ),
        in_specs=[
            pl.BlockSpec((dec_rows, depth), lambda i: (0, i)),
            pl.BlockSpec((1, depth), lambda i: (0, i)),
        ]
        + weight_blocks(0),
        out_specs=(fixed((dec_rows, query_width)), fixed((dec_rows, 128))),
        compiler_params=limits(56),
    )(dec_hidden, gain_view, *weights)
    message = pl.pallas_call(
        functools.partial(query_last_kernel, dec_width),
        grid=(last_steps,),
        out_shape=jax.ShapeDtypeStruct((dec_rows + 16, query_width), BF16),
        in_specs=[
            pl.BlockSpec((dec_rows, depth), lambda i: (0, i + first_steps)),
            pl.BlockSpec((1, depth), lambda i: (0, i + first_steps)),
            *weight_blocks(first_steps),
            fixed((dec_rows, query_width)),
            fixed((dec_rows, 128)),
            fixed((1, HD)),
            fixed((1, dec_rows)),
            fixed((1, dec_rows)),
        ],
        out_specs=fixed((dec_rows + 16, query_width)),
        scratch_shapes=[pltpu.VMEM((dec_rows, query_width), F32), pltpu.VMEM((dec_rows, 128), F32)],
        compiler_params=limits(56),
    )(
        dec_hidden,
        gain_view,
        *weights,
        begun,
        squares,
        query_gain.reshape(1, -1),
        image_of_row.reshape(1, -1),
        valid_count.reshape(1, -1),
    )

    owner = lax.axis_index("c") * XS + lax.axis_index("x")
    share = lax.dynamic_slice_in_dim(enc_out, owner * SHARE, SHARE, axis=0)
    share = jnp.pad(share, ((0, 24 - SHARE), (0, 0)))
    gain_row = enc_gain.reshape(1, -1)
    pieces = gather_tensor(jnp.concatenate([own, share], axis=0))
    qkv_weight = enc_qkv.transpose(0, 2, 1)
    row_shape = jax.ShapeDtypeStruct((rows, width), BF16)
    kv, share, normed, raw = pl.pallas_call(
        qkv_kernel,
        out_shape=(
            jax.ShapeDtypeStruct((4 * EHD, rows), BF16),
            jax.ShapeDtypeStruct((TENSOR * SHARE, 2 * HD), BF16),
            row_shape,
            row_shape,
        ),
        in_specs=[smem()] + vmem(TENSOR + 3),
        out_specs=tuple(vmem(4)),
        scratch_shapes=[pltpu.VMEM((TENSOR * SLOT, width), BF16)],
        compiler_params=limits(16),
    )(me, *pieces, gain_row, qkv_weight, cross_kv)
    kv_pieces = gather_xc(kv)
    shares = gather_xc(share)
    q, base = pl.pallas_call(
        local_kernel,
        out_shape=(
            jax.ShapeDtypeStruct((2, rows, EHD), BF16),
            jax.ShapeDtypeStruct((rows, 2 * HD), F32),
        ),
        in_specs=vmem(4),
        out_specs=tuple(vmem(2)),
        compiler_params=limits(12),
    )(normed, raw, qkv_weight, cross_kv)
    every_query = [message]
    for k in range(1, ZH):
        every_query.append(xor_permute(message, "zh", ZH, k))

    attended = pl.pallas_call(
        encoder_kernel,
        out_shape=jax.ShapeDtypeStruct((2 * EHD, rows), BF16),
        in_specs=vmem(9),
        out_specs=vmem(1)[0],
        scratch_shapes=[pltpu.VMEM((2, rows, 8 * rows), F32)],
        compiler_params=limits(20),
    )(q, *kv_pieces)
    attended_pieces = gather_tensor(attended)
    folded = pl.pallas_call(
        fold_kernel,
        out_shape=jax.ShapeDtypeStruct((TENSOR, 2 * EHD, 2 * HD), BF16),
        in_specs=[smem()] + vmem(8),
        out_specs=vmem(1)[0],
        scratch_shapes=[pltpu.VMEM((TENSOR * 2 * EHD, 2 * HD), BF16)],
        compiler_params=limits(16),
    )(place, *shares)
    slab = pl.pallas_call(
        cross_kernel,
        out_shape=jax.ShapeDtypeStruct((rows, 2 * HD), BF16),
        in_specs=[smem()] + vmem(TENSOR + 3),
        out_specs=vmem(1)[0],
        compiler_params=limits(12),
    )(me, *attended_pieces, folded, base, key_gain.reshape(1, -1))
    slabs = gather_xc(slab)
    result = None
    for k in (2, 1, 3, 0):
        out = pl.pallas_call(
            decode_kernel,
            out_shape=jax.ShapeDtypeStruct((dec_rows, 4 * HD), BF16),
            in_specs=[smem()] + vmem(9),
            out_specs=vmem(1)[0],
            compiler_params=limits(12),
        )(place, every_query[k], *slabs)
        if k:
            out = xor_permute(out, "zh", ZH, k)
        result = out if result is None else result + out
    return result


def solution(mesh):
    parts = Mesh(mesh.devices.reshape(ZH, CORES, YS, ZL, XS), ("zh", "c", "y", "zl", "x"))
    group, tensor, seq = ("zh", "c"), ("y", "zl"), ("x",)
    in_specs = (
        P(group + tensor + seq, None),
        P(),
        P(None, None, tensor),
        P(tensor, None),
        P(None, tensor),
        P(),
        P(group + seq, None),
        P(),
        P(None, tensor),
        P(),
        P(group + seq),
        P(group + seq),
    )
    out_specs = P(group + seq, tensor)

    return jax.shard_map(
        on_device, mesh=parts, in_specs=in_specs, out_specs=out_specs, check_vma=False
    )
```

```python
import functools
import math

import jax
import jax.numpy as jnp
from jax import lax
from jax.experimental import pallas as pl
from jax.experimental.pallas import tpu as pltpu
from jax.sharding import Mesh
from jax.sharding import PartitionSpec as P

EHD = 80
HD = 128
EPSILON = 1e-05
F32 = jnp.float32
BF16 = jnp.bfloat16
ZH, CORES, YS, ZL, XS = 4, 2, 4, 2, 4
SHARE, SLOT, STREAMS = 20, 32, 4
TENSOR_ORDER, X_ORDER = (5, 7, 3, 4, 6, 2, 1), (2, 3, 1)
TENSOR = YS * ZL
NT = (((1,), (1,)), ((), ()))


def vmem(count):
    return [pl.BlockSpec(memory_space=pltpu.VMEM)] * count


def smem():
    return pl.BlockSpec(memory_space=pltpu.SMEM)


def xor_permute(values, axes, size, step):
    return lax.ppermute(values, axes, [(i, i ^ step) for i in range(size)])


def image_permute(values):
    pairs = []
    for zh in range(ZH):
        for y in range(YS):
            for zl in range(ZL):
                image, slot = (y % 2) * 2 + zl, (y // 2) * ZH + zh
                pairs.append(((zh * YS + y) * ZL + zl, image * TENSOR + slot))
    return lax.ppermute(values, ("zh", "y", "zl"), pairs)


def qkv_kernel(me_ref, *refs):
    pieces, refs = refs[:TENSOR], refs[TENSOR:]
    gain_ref, weight_ref, cross_ref, q_ref, kv_ref, base_ref, normed, raw, out_rows = refs
    me = me_ref[0]
    rows = raw.shape[0] // TENSOR
    for step in range(TENSOR):
        piece = pieces[step][:rows, :]
        values = piece.astype(F32)
        mean_value = jnp.mean(values, axis=-1, keepdims=True)
        centered = values - mean_value
        variance = jnp.mean(centered * centered, axis=-1, keepdims=True)
        result = centered * lax.rsqrt(variance + EPSILON) * gain_ref[...]
        place = pl.ds(pl.multiple_of(jnp.bitwise_xor(me, step) * rows, rows), rows)
        normed[place, :] = result.astype(BF16)
        raw[place, :] = piece
        share = pieces[step][rows:, :]
        fill = jnp.zeros((SLOT - share.shape[0], share.shape[1]), BF16)
        place = pl.ds(pl.multiple_of(jnp.bitwise_xor(me, step) * SLOT, SLOT), SLOT)
        out_rows[place, :] = jnp.concatenate([share, fill], axis=0)
    x = normed[...]
    width = 2 * EHD
    for part in range(2):
        out = lax.dot_general(weight_ref[1 + part], x, NT, preferred_element_type=F32)
        kv_ref[part * width : (part + 1) * width, :] = out.astype(BF16)
    q = lax.dot_general(x, weight_ref[0], NT, preferred_element_type=F32)
    for head in range(2):
        q_ref[head] = q[:, head * EHD : (head + 1) * EHD].astype(BF16)
    cross = cross_ref[...]
    fold = jnp.dot(out_rows[...], cross, preferred_element_type=F32)
    row = lax.broadcasted_iota(jnp.int32, (TENSOR * SHARE, TENSOR * SLOT), 0)
    column = lax.broadcasted_iota(jnp.int32, (TENSOR * SHARE, TENSOR * SLOT), 1)
    chosen = (column == row + ((row * 3277) >> 16) * (SLOT - SHARE)).astype(F32).astype(BF16)
    fold = jnp.dot(chosen, fold.astype(BF16), preferred_element_type=F32)
    kv_ref[4 * EHD :, :] = fold.astype(BF16)
    base_ref[...] = jnp.dot(raw[...], cross, preferred_element_type=F32)


def encoder_kernel(q_ref, *refs):
    count = 8
    pieces, (out_ref, scores) = refs[:count], refs[count:]
    rows = q_ref.shape[1]
    scale = 1.0 / math.sqrt(EHD)
    for head in range(2):
        q = q_ref[head]
        top = None
        for j in range(count):
            s = jnp.dot(q, pieces[j][head * EHD : (head + 1) * EHD, :], preferred_element_type=F32)
            scores[head, :, j * rows : (j + 1) * rows] = s
            part = jnp.maximum(s[:, :128], s[:, 128:])
            top = part if top is None else jnp.maximum(top, part)
        top = jnp.max(top, axis=-1, keepdims=True)
        mix = jnp.zeros((rows, EHD), F32)
        total = jnp.zeros((rows, 128), F32)
        low = 2 * EHD + head * EHD
        for j in range(count):
            p = jnp.exp((scores[head, :, j * rows : (j + 1) * rows] - top) * scale)
            total = total + (p[:, :128] + p[:, 128:])
            mix = mix + lax.dot_general(
                p.astype(BF16), pieces[j][low : low + EHD, :], NT, preferred_element_type=F32
            )
        attended = mix / jnp.sum(total, axis=-1, keepdims=True)
        out_ref[head * EHD : (head + 1) * EHD, :] = attended.T.astype(BF16)


def fold_kernel(place_ref, *refs):
    pieces, (out_ref, stacked) = refs[:8], refs[8:]
    x, c = place_ref[1], place_ref[2]
    size = TENSOR * SHARE
    for k in range(8):
        owner = jnp.bitwise_xor(c, k // 4) * 4 + jnp.bitwise_xor(x, k % 4)
        low = pl.multiple_of(owner * size, size)
        stacked[pl.ds(low, size), :] = pieces[k][4 * EHD :, :]
    for t in range(TENSOR):
        row = lax.broadcasted_iota(jnp.int32, (size, 8 * size), 0)
        column = lax.broadcasted_iota(jnp.int32, (size, 8 * size), 1)
        owner = (row * 3277) >> 16
        source = owner * (size - SHARE) + row + t * SHARE
        chosen = (column == source).astype(F32).astype(BF16)
        out = jnp.dot(chosen, stacked[...], preferred_element_type=F32)
        out_ref[t] = out.astype(BF16)


def cross_kernel(me_ref, *refs):
    pieces, (weight_ref, base_ref, gain_ref, out_ref) = refs[:TENSOR], refs[TENSOR:]
    me = me_ref[0]
    proj = base_ref[...]
    for step in range(TENSOR):
        weight = weight_ref[jnp.bitwise_xor(me, step)]
        proj = proj + lax.dot_general(
            pieces[step][...], weight, (((0,), (0,)), ((), ())), preferred_element_type=F32
        )
    keys = proj[:, :HD]
    square_mean = jnp.mean(keys * keys, axis=-1, keepdims=True)
    keys = keys * lax.rsqrt(square_mean + EPSILON) * gain_ref[...]
    out_ref[:, :HD] = keys.astype(BF16)
    out_ref[:, HD:] = proj[:, HD:].astype(BF16)


def query_part(x_ref, gain_ref, weights, total, square):
    depth = weights[0].shape[0]
    out, squares = total[...], square[...]
    for k, weight_ref in enumerate(weights):
        columns = slice(k * depth, (k + 1) * depth)
        x = x_ref[:, columns].astype(F32)
        for low in range(0, depth, 128):
            part = x[:, low : low + 128]
            squares = squares + part * part
        scaled = (x * gain_ref[:, columns]).astype(BF16)
        out = out + jnp.dot(scaled, weight_ref[...], preferred_element_type=F32)
    total[...], square[...] = out, squares


def query_first_kernel(x_ref, gain_ref, *refs):
    weights, (total, square) = refs[:STREAMS], refs[STREAMS:]

    @pl.when(pl.program_id(0) == 0)
    def _():
        total[...] = jnp.zeros_like(total)
        square[...] = jnp.zeros_like(square)

    query_part(x_ref, gain_ref, weights, total, square)


def query_last_kernel(width, x_ref, gain_ref, *refs):
    weights, refs = refs[:STREAMS], refs[STREAMS:]
    begun, squares, head_gain_ref, image_ref, count_ref, out_ref, total, square = refs
    rows = x_ref.shape[0]

    @pl.when(pl.program_id(0) == 0)
    def _():
        total[...] = begun[...]
        square[...] = squares[...]

    query_part(x_ref, gain_ref, weights, total, square)

    @pl.when(pl.program_id(0) == pl.num_programs(0) - 1)
    def _():
        inverse = lax.rsqrt(jnp.sum(square[...], axis=-1, keepdims=True) / width + EPSILON)
        for head in range(4):
            q = total[:, head * HD : (head + 1) * HD] * inverse
            mean = jnp.mean(q * q, axis=-1, keepdims=True)
            q = q * lax.rsqrt(mean + EPSILON) * head_gain_ref[...] / math.sqrt(HD)
            out_ref[:rows, head * HD : (head + 1) * HD] = q.astype(BF16)
        count = count_ref[...]
        extra = jnp.concatenate([image_ref[...], count >> 4, count & 15], axis=0)
        extra = jnp.concatenate([extra, jnp.zeros((13, rows), jnp.int32)], axis=0)
        out_ref[rows:, :rows] = extra.astype(F32).astype(BF16)
        out_ref[rows:, rows:] = jnp.zeros((16, out_ref.shape[1] - rows), BF16)


def decode_rows(q, limit, first, slabs):
    keys = slabs[0].shape[0]
    lane = lax.broadcasted_iota(jnp.int32, (1, keys), 1)
    base = ((lane >> 5) & 3) * 512 + (lane >> 7) * 128 + (lane & 31)
    mix = jnp.zeros((q.shape[0], HD), F32)
    total = jnp.zeros((q.shape[0], 128), F32)
    for j in range(8):
        pos = (base + first[j]).astype(F32)
        s = lax.dot_general(q, slabs[j][:, :HD], NT, preferred_element_type=F32)
        w = jnp.where(pos < limit, jnp.exp(s), 0.0)
        total = total + (w[:, :128] + w[:, 128:])
        mix = mix + jnp.dot(w.astype(BF16), slabs[j][:, HD:], preferred_element_type=F32)
    total = jnp.sum(total, axis=-1, keepdims=True)
    return (mix / jnp.where(total > 0.0, total, 1.0)).astype(BF16)


def decode_kernel(place_ref, query_ref, *refs):
    slabs, out_ref = refs[:8], refs[8]
    rows = out_ref.shape[0]
    few = rows // 2
    zh, x, c = place_ref[0], place_ref[1], place_ref[2]
    first = [jnp.bitwise_xor(c, j // 4) * 256 + jnp.bitwise_xor(x, j % 4) * 32 for j in range(8)]
    extra = query_ref[rows : rows + 8, :HD].astype(F32)
    mine = extra[0:1] == zh.astype(F32)
    limit = jnp.where(mine, extra[1:2] * 16.0 + extra[2:3], 0.0)
    member = mine.astype(F32)
    count = jnp.sum(member)

    below = lax.broadcasted_iota(jnp.int32, (rows, rows), 0)
    below = below < lax.broadcasted_iota(jnp.int32, (rows, rows), 1)
    rank = jnp.dot(
        jnp.broadcast_to(member, (8, rows)).astype(BF16),
        below.astype(F32).astype(BF16),
        preferred_element_type=F32,
    )[0:1]
    out_ref[...] = jnp.zeros_like(out_ref)

    def half(step, carry):
        slot = lax.broadcasted_iota(jnp.int32, (few, rows), 0) + step * few
        chosen = jnp.where(rank == slot.astype(F32), member, 0.0)
        picked = chosen.astype(BF16)
        q = jnp.dot(picked, query_ref[:rows, :], preferred_element_type=F32).astype(BF16)
        q = jnp.concatenate([q[:, head * HD : (head + 1) * HD] for head in range(4)], axis=0)
        bound = jnp.sum(chosen * limit, axis=-1, keepdims=True)
        out = decode_rows(q, jnp.concatenate([bound] * 4, axis=0), first, slabs)
        out = jnp.concatenate([out[head * few : (head + 1) * few] for head in range(4)], axis=1)
        back = jnp.dot(chosen.T.astype(BF16), out, preferred_element_type=F32)
        out_ref[...] = (out_ref[...].astype(F32) + back).astype(BF16)
        return carry

    lax.fori_loop(0, jnp.where(count > few, 2, 1), half, 0)


def limits(mib):
    return pltpu.CompilerParams(vmem_limit_bytes=mib << 20)


def gather_xc(piece):
    along_x = {0: piece}
    for k in X_ORDER:
        along_x[k] = xor_permute(piece, "x", XS, k)
    along_x = [along_x[k] for k in range(XS)]
    return along_x + [xor_permute(value, "c", CORES, 1) for value in along_x]


def gather_tensor(piece):
    pieces = {0: piece}
    for k in TENSOR_ORDER:
        pieces[k] = xor_permute(piece, ("y", "zl"), TENSOR, k)
    return [pieces[k] for k in range(TENSOR)]


def on_device(
    patches,
    enc_gain,
    enc_qkv,
    enc_out,
    cross_kv,
    key_gain,
    dec_hidden,
    dec_gain,
    query_weight,
    query_gain,
    image_of_row,
    valid_count,
):
    tensor_index = (lax.axis_index("y") * ZL + lax.axis_index("zl")).astype(jnp.int32)
    me = tensor_index.reshape(1)
    place = jnp.stack([lax.axis_index("zh"), lax.axis_index("x"), lax.axis_index("c")]).astype(
        jnp.int32
    )
    patch_rows, width = patches.shape
    rows = patch_rows * TENSOR
    own = image_permute(patches)

    dec_rows = dec_hidden.shape[0]
    depth, first_steps, last_steps = 1024, 4, 4
    dec_width, query_width = query_weight.shape
    fixed = lambda shape: pl.BlockSpec(shape, lambda i: (0, 0))
    gain_view = dec_gain.reshape(1, -1)
    weights = [query_weight] * STREAMS

    def weight_blocks(begin):
        shape = (depth // STREAMS, query_width)
        return [
            pl.BlockSpec(shape, lambda i, k=k: ((i + begin) * STREAMS + k, 0))
            for k in range(STREAMS)
        ]

    begun, squares = pl.pallas_call(
        query_first_kernel,
        grid=(first_steps,),
        out_shape=(
            jax.ShapeDtypeStruct((dec_rows, query_width), F32),
            jax.ShapeDtypeStruct((dec_rows, 128), F32),
        ),
        in_specs=[
            pl.BlockSpec((dec_rows, depth), lambda i: (0, i)),
            pl.BlockSpec((1, depth), lambda i: (0, i)),
        ]
        + weight_blocks(0),
        out_specs=(fixed((dec_rows, query_width)), fixed((dec_rows, 128))),
        compiler_params=limits(56),
    )(dec_hidden, gain_view, *weights)
    message = pl.pallas_call(
        functools.partial(query_last_kernel, dec_width),
        grid=(last_steps,),
        out_shape=jax.ShapeDtypeStruct((dec_rows + 16, query_width), BF16),
        in_specs=[
            pl.BlockSpec((dec_rows, depth), lambda i: (0, i + first_steps)),
            pl.BlockSpec((1, depth), lambda i: (0, i + first_steps)),
            *weight_blocks(first_steps),
            fixed((dec_rows, query_width)),
            fixed((dec_rows, 128)),
            fixed((1, HD)),
            fixed((1, dec_rows)),
            fixed((1, dec_rows)),
        ],
        out_specs=fixed((dec_rows + 16, query_width)),
        scratch_shapes=[pltpu.VMEM((dec_rows, query_width), F32), pltpu.VMEM((dec_rows, 128), F32)],
        compiler_params=limits(56),
    )(
        dec_hidden,
        gain_view,
        *weights,
        begun,
        squares,
        query_gain.reshape(1, -1),
        image_of_row.reshape(1, -1),
        valid_count.reshape(1, -1),
    )

    owner = lax.axis_index("c") * XS + lax.axis_index("x")
    share = lax.dynamic_slice_in_dim(enc_out, owner * SHARE, SHARE, axis=0)
    share = jnp.pad(share, ((0, 24 - SHARE), (0, 0)))
    gain_row = enc_gain.reshape(1, -1)
    pieces = gather_tensor(jnp.concatenate([own, share], axis=0))
    q, kv, base = pl.pallas_call(
        qkv_kernel,
        out_shape=(
            jax.ShapeDtypeStruct((2, rows, EHD), BF16),
            jax.ShapeDtypeStruct((4 * EHD + TENSOR * SHARE, rows), BF16),
            jax.ShapeDtypeStruct((rows, 2 * HD), F32),
        ),
        in_specs=[smem()] + vmem(TENSOR + 3),
        out_specs=tuple(vmem(3)),
        scratch_shapes=[
            pltpu.VMEM((rows, width), BF16),
            pltpu.VMEM((rows, width), BF16),
            pltpu.VMEM((TENSOR * SLOT, width), BF16),
        ],
        compiler_params=limits(16),
    )(me, *pieces, gain_row, enc_qkv.transpose(0, 2, 1), cross_kv)
    kv_pieces = gather_xc(kv)
    every_query = [message]
    for k in range(1, ZH):
        every_query.append(xor_permute(message, "zh", ZH, k))

    attended = pl.pallas_call(
        encoder_kernel,
        out_shape=jax.ShapeDtypeStruct((2 * EHD, rows), BF16),
        in_specs=vmem(9),
        out_specs=vmem(1)[0],
        scratch_shapes=[pltpu.VMEM((2, rows, 8 * rows), F32)],
        compiler_params=limits(20),
    )(q, *kv_pieces)
    attended_pieces = gather_tensor(attended)
    folded = pl.pallas_call(
        fold_kernel,
        out_shape=jax.ShapeDtypeStruct((TENSOR, 2 * EHD, 2 * HD), BF16),
        in_specs=[smem()] + vmem(8),
        out_specs=vmem(1)[0],
        scratch_shapes=[pltpu.VMEM((TENSOR * 2 * EHD, 2 * HD), BF16)],
        compiler_params=limits(16),
    )(place, *kv_pieces)
    slab = pl.pallas_call(
        cross_kernel,
        out_shape=jax.ShapeDtypeStruct((rows, 2 * HD), BF16),
        in_specs=[smem()] + vmem(TENSOR + 3),
        out_specs=vmem(1)[0],
        compiler_params=limits(12),
    )(me, *attended_pieces, folded, base, key_gain.reshape(1, -1))
    slabs = gather_xc(slab)
    result = None
    for k in (2, 1, 3, 0):
        out = pl.pallas_call(
            decode_kernel,
            out_shape=jax.ShapeDtypeStruct((dec_rows, 4 * HD), BF16),
            in_specs=[smem()] + vmem(9),
            out_specs=vmem(1)[0],
            compiler_params=limits(12),
        )(place, every_query[k], *slabs)
        if k:
            out = xor_permute(out, "zh", ZH, k)
        result = out if result is None else result + out
    return result


def solution(mesh):
    parts = Mesh(mesh.devices.reshape(ZH, CORES, YS, ZL, XS), ("zh", "c", "y", "zl", "x"))
    group, tensor, seq = ("zh", "c"), ("y", "zl"), ("x",)
    in_specs = (
        P(group + tensor + seq, None),
        P(),
        P(None, None, tensor),
        P(tensor, None),
        P(None, tensor),
        P(),
        P(group + seq, None),
        P(),
        P(None, tensor),
        P(),
        P(group + seq),
        P(group + seq),
    )
    out_specs = P(group + seq, tensor)

    return jax.shard_map(
        on_device, mesh=parts, in_specs=in_specs, out_specs=out_specs, check_vma=False
    )
```
